512 devices in a mesh: grp: 16 (over x_lo, y, core), tok: 32 (over x_hi, z).
Axes of the slice: x: 4 (x_hi: 2, x_lo: 2; x = x_hi * 2 + x_lo), y: 4, z: 16, core: 2. Of those that a mesh axis runs over, the one named last changes fastest.
Arguments:
- probe_states: bfloat16 [1024, 2048], P('tok'), may hold values from -40 to 40
- norm_gain: float32 [2048], replicated, may hold values from 0.1 to 1.9
- gate_weight: bfloat16 [98304, 2048], P(('grp', 'tok')), may hold values from -1 to 1
- up_weight: bfloat16 [98304, 2048], P(('grp', 'tok')), may hold values from -1 to 1
- down_weight: bfloat16 [98304, 2048], P(('grp', 'tok')), may hold values from -1 to 1
- route_weight: float32 [512, 256], P(('grp', 'tok')), may hold values from 0.02 to 1
Outputs:
- features: bfloat16 [131072, 2048], P(('grp', 'tok'))
- cka: float32 [128, 128], replicated
The draws below stay inside these ranges and needn't reach their ends.
All inputs are finite; a program needn't handle non-finite values.
Results may differ from the reference program's by a relative error of at most 0.0015.
The reference program's roundings to bfloat16 on the way (of `normed`, `hidden` and `centered`) count: a program that leaves them out, or rounds other values in their place, can miss the bound.
Values may be sent and summed in bfloat16 or wider, within the bound.
A program may use at most 64 MiB of HBM per device.

```python
import math
import jax
import jax.numpy as jnp
from jax import lax

D = 2048
FF = 768
TOKENS = 1024
EXPERTS = 128


def fresh_noise(key, shape):
    return jnp.clip(jax.random.normal(key, shape, jnp.float32), -6.0, 6.0)


def cluster_mix(key):
    clusters = jax.random.randint(jax.random.fold_in(key, 101), (EXPERTS,), 0, 4).astype(jnp.int32)
    mixing = jax.random.uniform(jax.random.fold_in(key, 102), (EXPERTS,), jnp.float32, 0.35, 0.95)
    return (clusters, mixing)


def clustered_weight(key, salt_value, fan_count):
    clusters, mixing = cluster_mix(key)
    shared = fresh_noise(jax.random.fold_in(key, salt_value), (4, FF, D))
    own_key = jax.random.fold_in(key, salt_value + 1)

    def one_slab(inputs):
        expert_index, cluster_index, weight_mix = inputs
        common = lax.dynamic_index_in_dim(shared, cluster_index, 0, keepdims=False)
        private = fresh_noise(jax.random.fold_in(own_key, expert_index), (FF, D))
        mixed = weight_mix * common + jnp.sqrt(1.0 - weight_mix * weight_mix) * private
        return mixed / jnp.sqrt(jnp.float32(fan_count))
    slabs = lax.map(one_slab, (jnp.arange(EXPERTS, dtype=jnp.int32), clusters, mixing))
    return slabs.reshape(EXPERTS * FF, D).astype(jnp.bfloat16)


def draw_gate_weight(key, part):
    return clustered_weight(key, 201, D)


def draw_up_weight(key, part):
    return clustered_weight(key, 301, D)


def draw_down_weight(key, part):
    return clustered_weight(key, 401, FF)


def draw_probe_states(key, part):
    directions = jax.random.normal(jax.random.fold_in(key, 501), (4, 2, D), jnp.float32)
    loadings = jax.random.normal(jax.random.fold_in(key, 502), (TOKENS, 2), jnp.float32)
    private = fresh_noise(jax.random.fold_in(key, 503), (TOKENS, D))
    block_of_row = (jnp.arange(TOKENS, dtype=jnp.int32) // (TOKENS // 4)).astype(jnp.int32)
    chosen = directions[block_of_row]
    structured = (loadings[:, 0:1] * chosen[:, 0, :] + loadings[:, 1:2] * chosen[:, 1, :]) / jnp.sqrt(jnp.float32(2.0))
    states = jnp.sqrt(jnp.float32(0.4)) * structured + jnp.sqrt(jnp.float32(0.6)) * private
    return jnp.clip(states, -40.0, 40.0).astype(jnp.bfloat16)


def level_of(key, extent, cuts, low, high):
    factor_of = 1.0
    for position, blocks in cuts:
        draws = jax.random.uniform(jax.random.fold_in(jax.random.fold_in(key, 6), position), (blocks,), jnp.float32, low / len(cuts), high / len(cuts))
        factor_of = factor_of * jnp.repeat(jnp.exp(draws), extent[position] // blocks).reshape((-1,) + (1,) * (len(extent) - 1 - position))
    return factor_of


def setup_inputs(seed: int = 0) -> dict:
    splits = jax.random.split(jax.random.key(seed), 7)
    return {
        "probe_states": draw_probe_states(jax.random.fold_in(splits[6], 71), 0),
        "norm_gain": jnp.clip(1.0 + 0.18 * jax.random.normal(splits[1], (D,), jnp.float32), 0.1, 1.9),
        "gate_weight": draw_gate_weight(jax.random.fold_in(splits[6], 71), 0),
        "up_weight": draw_up_weight(jax.random.fold_in(splits[6], 71), 0),
        "down_weight": draw_down_weight(jax.random.fold_in(splits[6], 71), 0),
        "route_weight": jnp.clip(jnp.exp(math.log(1.0) - 3.912023 * jax.random.uniform(splits[5], (EXPERTS * 4, TOKENS // 4), jnp.float32) ** level_of(splits[5], (EXPERTS * 4, TOKENS // 4), ((0, 512),), -0.2, 0.2)), 0.02, 1.0),
    }


def reference(probe_states, norm_gain, gate_weight, up_weight, down_weight, route_weight):
    states = probe_states.astype(jnp.float32)
    scaled = states * lax.rsqrt(lax.optimization_barrier(jnp.mean(states * states, axis=1, keepdims=True)) + 1e-06) * norm_gain
    normed = scaled.astype(jnp.bfloat16)
    gates = gate_weight.reshape(EXPERTS, FF, D)
    uppers = up_weight.reshape(EXPERTS, FF, D)
    downs = down_weight.reshape(EXPERTS, FF, D)
    routes = route_weight.reshape(EXPERTS, TOKENS)
    contract = (((1,), (1,)), ((), ()))

    def one_expert(weights):
        w_gate, w_up, w_down, route_row = weights
        gate = lax.dot_general(normed, w_gate, contract, preferred_element_type=jnp.float32)
        upward = lax.dot_general(normed, w_up, contract, preferred_element_type=jnp.float32)
        hidden = (jax.nn.silu(gate) * upward).astype(jnp.bfloat16)
        output = jnp.dot(hidden, w_down, preferred_element_type=jnp.float32)
        feats = (output * route_row[:, None]).astype(jnp.bfloat16)
        column_mean = lax.optimization_barrier(jnp.sum(feats, axis=0, dtype=jnp.float32)) / TOKENS
        projection = lax.optimization_barrier(jnp.sum(feats.astype(jnp.float32) * column_mean, axis=1))
        mean_square = jnp.sum(column_mean * column_mean)
        gram = lax.dot_general(feats, feats, contract, preferred_element_type=jnp.float32)
        centered = (gram - projection[:, None] - projection[None, :] + mean_square).astype(jnp.bfloat16)
        return (feats, centered.reshape(-1))
    feats_all, flat = lax.map(one_expert, (gates, uppers, downs, routes))
    pair_totals = jnp.dot(flat, flat.T, preferred_element_type=jnp.float32)
    diagonal = jnp.diagonal(pair_totals)
    cka = pair_totals / jnp.sqrt(diagonal[:, None] * diagonal[None, :])
    return (feats_all.reshape(EXPERTS * TOKENS, D), cka)
```

```python
import functools

import jax
import jax.numpy as jnp
from jax import lax
from jax.experimental import pallas as pl
from jax.experimental.pallas import tpu as pltpu
from jax.sharding import PartitionSpec as P

F32 = jnp.float32
BF16 = jnp.bfloat16
NT = (((1,), (1,)), ((), ()))
MESH = pl.DeviceIdType.MESH
VM = pl.BlockSpec(memory_space=pltpu.VMEM)


class Place:
    def __init__(self):
        self.g = lax.axis_index("grp")
        self.t = lax.axis_index("tok")
        self.xl = self.g // 8
        self.y = (self.g // 2) % 4
        self.c = self.g % 2
        self.xh = self.t // 16
        self.z = self.t % 16
        self.q = self.t % 4
        self.h = self.t // 4
        self.base = self.h * 4
        self.owner_q = 1 + self.c
        self.owner = self.base + self.owner_q
        self.rank = (self.q + 4 - self.owner_q) % 4

    def at_y(self, step):
        return (self.xl * 8 + ((self.y + step) % 4) * 2 + self.c, self.t)

    def at_x(self, step):
        x = (self.xh * 2 + self.xl + step) % 4
        return ((x % 2) * 8 + self.y * 2 + self.c, (x // 2) * 16 + self.z)

    def at_z(self, step):
        return (self.g, self.xh * 16 + (self.z + step) % 16)

    def at_core(self):
        return (self.xl * 8 + self.y * 2 + 1 - self.c, self.t)


def push(src, dst, send, recv, device):
    return pltpu.make_async_remote_copy(
        src_ref=src, dst_ref=dst, send_sem=send, recv_sem=recv, device_id=device, device_id_type=MESH
    )


def greet(devices):
    barrier = pltpu.get_barrier_semaphore()
    for device in devices:
        pl.semaphore_signal(barrier, inc=1, device_id=device, device_id_type=MESH)
    return barrier


def expert_kernel(
    x_ref, gain_ref, gate_ref, up_ref, down_ref, route_ref,
    feat_ref,
    nrm, tok, hid, downs, routes,
    z_send, z_recv, y_send, y_recv, x_send, x_recv, c_send, c_recv, w_send, w_recv, d_send, d_recv,
):
    me = Place()
    partners = [me.at_z(s) for s in range(1, 16)]
    partners += [me.at_x(1), me.at_x(3), me.at_y(1), me.at_y(3), me.at_core()]
    barrier = greet(partners)

    states = x_ref[...].astype(F32)
    scale = lax.rsqrt(jnp.mean(states * states, axis=1, keepdims=True) + 1e-06)
    nrm[...] = (states * scale * gain_ref[...]).astype(BF16)
    group = me.c * 8 + me.xl * 4 + me.y
    rows = pl.ds(pl.multiple_of(me.t * 32, 32), 32)
    columns = pl.ds(pl.multiple_of(group * 128, 128), 128)
    tok[rows, columns] = nrm[:, columns]
    pl.semaphore_wait(barrier, len(partners))

    sends = []

    def start(copy):
        copy.start()
        sends.append(copy)

    for s in range(1, 16):
        start(push(nrm.at[:, columns], tok.at[rows, columns], z_send.at[s], z_recv.at[s], me.at_z(s)))
    for s in range(1, 16):
        source = pl.ds(pl.multiple_of((me.xh * 16 + (me.z + 16 - s) % 16) * 32, 32), 32)
        push(nrm.at[:, columns], tok.at[source, columns], z_send.at[s], z_recv.at[s], me.at_z(s)).wait_recv()

    def spot(step_x, y):
        x = (me.xh * 2 + me.xl + step_x) % 4
        row = pl.multiple_of((x // 2) * 512, 512)
        return row, pl.multiple_of((me.c * 8 + (x % 2) * 4 + y) * 128, 128)

    def y_copy(part, direction, source_step, slot):
        row, col = spot(0, (me.y + source_step) % 4)
        start_row, count = ((0, 512), (0, 256), (256, 256))[part]
        block = tok.at[pl.ds(row + start_row, count), pl.ds(col, 128)]
        return push(block, block, y_send.at[slot], y_recv.at[slot], me.at_y(direction))

    def x_copy(slot, direction, source_step, y):
        row, col = spot(source_step, y)
        block = tok.at[pl.ds(row, 512), pl.ds(col, 128)]
        return push(block, block, x_send.at[slot, y], x_recv.at[slot, y], me.at_x(direction))

    def core_copy(step_x, core):
        x = (me.xh * 2 + me.xl + step_x) % 4
        row = pl.multiple_of((x // 2) * 512, 512)
        col = pl.multiple_of((core * 8 + (x % 2) * 4) * 128, 128)
        block = tok.at[pl.ds(row, 512), pl.ds(col, 512)]
        return push(block, block, c_send.at[step_x], c_recv.at[step_x], me.at_core())

    start(y_copy(0, 1, 0, 0))
    start(y_copy(0, 3, 0, 1))
    start(x_copy(0, 1, 0, me.y))
    start(x_copy(1, 3, 0, me.y))

    owner = (me.g, me.owner)
    slot = (me.rank + 3) % 4
    is_owner = me.rank == 0
    down_copy = push(down_ref, downs.at[slot], w_send.at[0], w_recv.at[slot, 0], owner)
    route_copy = push(route_ref, routes.at[me.q], w_send.at[1], w_recv.at[slot, 1], owner)

    @pl.when(jnp.logical_not(is_owner))
    def _():
        down_copy.start()
        route_copy.start()

    y_copy(0, 1, 3, 0).wait_recv()
    start(y_copy(1, 1, 3, 2))
    start(x_copy(0, 1, 0, (me.y + 3) % 4))
    start(x_copy(1, 3, 0, (me.y + 3) % 4))
    y_copy(0, 3, 1, 1).wait_recv()
    start(y_copy(2, 3, 1, 3))
    start(x_copy(0, 1, 0, (me.y + 1) % 4))
    start(x_copy(1, 3, 0, (me.y + 1) % 4))
    y_copy(1, 1, 2, 2).wait_recv()
    y_copy(2, 3, 2, 3).wait_recv()
    start(x_copy(0, 1, 0, (me.y + 2) % 4))
    start(x_copy(1, 3, 0, (me.y + 2) % 4))
    start(core_copy(0, me.c))

    for d in (0, 3, 1, 2):
        y = (me.y + d) % 4
        x_copy(0, 1, 3, y).wait_recv()
        x_copy(1, 3, 1, y).wait_recv()
        source = 3 - 2 * (y // 2)
        start(x_copy(2, 4 - source, source, y))
    start(core_copy(1, me.c))
    start(core_copy(3, me.c))

    def chunk_rows(k):
        block = (me.xh * 2 + k) % 4
        return block, pl.ds(pl.multiple_of(block * 256, 256), 256)

    def hidden_copy(k, source_slot):
        _, rows_k = chunk_rows(k)
        return push(
            hid.at[0, rows_k], hid.at[source_slot, rows_k], d_send.at[k], d_recv.at[source_slot, k], owner
        )

    def make_hidden(k):
        _, rows_k = chunk_rows(k)
        block = tok[rows_k, :]
        gate = lax.dot_general(block, gate_ref[...], NT, preferred_element_type=F32)
        upward = lax.dot_general(block, up_ref[...], NT, preferred_element_type=F32)
        hid[0, rows_k, :] = (gate / (1.0 + jnp.exp(-gate)) * upward).astype(BF16)

        @pl.when(jnp.logical_not(is_owner))
        def _():
            hidden_copy(k, me.rank).start()

    core_copy(0, 1 - me.c).wait_recv()
    core_copy(1 + 2 * me.xl, 1 - me.c).wait_recv()

    @pl.loop(0, 2)
    def _(k):
        make_hidden(k)

    for d in (0, 3, 1, 2):
        y = (me.y + d) % 4
        x_copy(2, 1, 2, y).wait_recv()
    start(core_copy(2, me.c))
    core_copy(3 - 2 * me.xl, 1 - me.c).wait_recv()
    core_copy(2, 1 - me.c).wait_recv()

    @pl.loop(2, 4)
    def _(k):
        make_hidden(k)

    @pl.when(is_owner)
    def _():
        for j in range(1, 4):
            device = (me.g, me.base + (me.owner_q + j) % 4)
            push(down_ref, downs.at[j - 1], w_send.at[0], w_recv.at[j - 1, 0], device).wait_recv()
            push(
                route_ref, routes.at[(me.owner_q + j) % 4], w_send.at[1], w_recv.at[j - 1, 1], device
            ).wait_recv()
        routes[me.q] = route_ref[...]

        @pl.loop(0, 4)
        def _(k):
            block, rows_k = chunk_rows(k)
            for j in range(1, 4):
                hidden_copy(k, j).wait_recv()
            route = routes[block]
            route_column = jnp.transpose(jnp.concatenate([route] * 16, axis=0))

            @pl.loop(0, 4)
            def _(n):
                cols = pl.ds(pl.multiple_of(n * 512, 512), 512)
                out = jnp.dot(hid[0, rows_k, :], down_ref[:, cols], preferred_element_type=F32)
                for j in range(1, 4):
                    out += jnp.dot(hid[j, rows_k, :], downs[j - 1, :, cols], preferred_element_type=F32)
                wide = jnp.concatenate([route_column] * 4, axis=1)
                feat_ref[rows_k, cols] = (out * wide).astype(BF16)

    @pl.when(jnp.logical_not(is_owner))
    def _():
        down_copy.wait_send()
        route_copy.wait_send()

        @pl.loop(0, 4)
        def _(k):
            hidden_copy(k, me.rank).wait_send()

    for copy in sends:
        copy.wait_send()


def make_features(probe_states, norm_gain, gate_weight, up_weight, down_weight, route_weight):
    dma = pltpu.SemaphoreType.DMA
    return pl.pallas_call(
        expert_kernel,
        out_shape=jax.ShapeDtypeStruct((1024, 2048), BF16),
        in_specs=[VM] * 6,
        out_specs=VM,
        scratch_shapes=[
            pltpu.VMEM((32, 2048), BF16),
            pltpu.VMEM((1024, 2048), BF16),
            pltpu.VMEM((4, 1024, 192), BF16),
            pltpu.VMEM((3, 192, 2048), BF16),
            pltpu.VMEM((4, 8, 256), F32),
            dma((16,)), dma((16,)), dma((4,)), dma((4,)), dma((3, 4)), dma((3, 4)),
            dma((4,)), dma((4,)), dma((2,)), dma((3, 2)), dma((4,)), dma((4, 4)),
        ],
        compiler_params=pltpu.CompilerParams(
            collective_id=0, has_side_effects=True, vmem_limit_bytes=48 << 20
        ),
        name="features",
    )(
        probe_states, norm_gain[None, :], gate_weight, up_weight, down_weight,
        jnp.broadcast_to(route_weight, (8, 256)),
    )


def exchange_kernel(cen_ref, out_ref, mid, a_send, a_recv, b_send, b_recv, local):
    me = Place()
    is_owner = me.rank == 0

    def over_grp(step):
        g = (me.g + step) % 16
        return g, (g, me.base + 1 + g % 2)

    def over_tok(step):
        h = (me.h + step) % 8
        return h, (me.g, h * 4 + me.owner_q)

    @pl.when(is_owner)
    def _():
        barrier = greet([over_grp(s)[1] for s in range(1, 16)] + [over_tok(s)[1] for s in range(1, 8)])
        pl.semaphore_wait(barrier, 22)

        def first(g_to, g_from, step, device):
            src = cen_ref.at[pl.ds(pl.multiple_of(g_to * 16, 16), 16), :]
            return push(src, mid.at[g_from], a_send.at[step], a_recv.at[step], device)

        def second(h_to, h_from, step, device):
            r = pl.ds(pl.multiple_of((h_to // 4) * 8, 8), 8)
            k = pl.ds(pl.multiple_of((h_to % 4) * 640, 128), 640)
            return push(mid.at[:, r, k], out_ref.at[:, h_from], b_send.at[step], b_recv.at[step], device)

        for s in range(1, 16):
            g, device = over_grp(s)
            first(g, me.g, s, device).start()
        mid[me.g] = cen_ref[pl.ds(pl.multiple_of(me.g * 16, 16), 16), :]
        for s in range(1, 16):
            g, device = over_grp(16 - s)
            first(me.g, g, s, device).wait_recv()
        for s in range(1, 8):
            h, device = over_tok(s)
            second(h, me.h, s, device).start()
        r = pl.ds(pl.multiple_of((me.h // 4) * 8, 8), 8)
        k = pl.ds(pl.multiple_of((me.h % 4) * 640, 128), 640)
        keep = pltpu.make_async_copy(mid.at[:, r, k], out_ref.at[:, me.h], local)
        keep.start()
        keep.wait()
        for s in range(1, 8):
            h, device = over_tok(8 - s)
            second(me.h, h, s, device).wait_recv()
        for s in range(1, 16):
            g, device = over_grp(s)
            first(g, me.g, s, device).wait_send()
        for s in range(1, 8):
            h, device = over_tok(s)
            second(h, me.h, s, device).wait_send()


def exchange(centered):
    dma = pltpu.SemaphoreType.DMA
    return pl.pallas_call(
        exchange_kernel,
        out_shape=jax.ShapeDtypeStruct((16, 8, 8, 640), BF16),
        in_specs=[VM],
        out_specs=VM,
        scratch_shapes=[
            pltpu.VMEM((16, 16, 2560), BF16),
            dma((16,)), dma((16,)), dma((8,)), dma((8,)), dma,
        ],
        compiler_params=pltpu.CompilerParams(collective_id=1, has_side_effects=True),
        name="exchange",
    )(centered)


def reduce_kernel(part_ref, feat_ref, total_ref, out_ref, first, mine, second, rows, f_send, f_recv,
                  a_send, a_recv, b_send, b_recv, c_send, c_recv):
    me = Place()
    is_owner = me.rank == 0

    def owner_of(g):
        return (g, me.base + 1 + g % 2)

    def over_tok(step):
        return (me.g, (me.t + step) % 32)

    def over_grp(step):
        return ((me.g + step) % 16, me.t)

    def in_quad(j):
        q = (me.owner_q + j) % 4
        return q, (me.g, me.base + q)

    barrier = greet([over_tok(s) for s in range(1, 32)] + [over_grp(s) for s in range(1, 16)])

    @pl.when(is_owner)
    def _():
        for s in range(1, 16, 2):
            pl.semaphore_signal(barrier, inc=1, device_id=owner_of((me.g + s) % 16), device_id_type=MESH)
        pl.semaphore_wait(barrier, 54)

    @pl.when(jnp.logical_not(is_owner))
    def _():
        pl.semaphore_wait(barrier, 46)

    def feature_copy(j):
        q, device = in_quad(j)
        src = feat_ref.at[pl.ds(pl.multiple_of(q * 256, 256), 256), :]
        return push(src, out_ref, f_send.at[j], f_recv, device)

    def a_copy(g_to, slot, device):
        src = part_ref.at[pl.ds(pl.multiple_of(g_to * 8, 8), 8), :]
        return push(src, first.at[slot], a_send.at[slot], a_recv.at[slot], device)

    @pl.when(is_owner)
    def _():
        for s in range(1, 16):
            g = (me.g + s) % 16
            a_copy(g, s, owner_of(g)).start()
        for j in range(1, 4):
            feature_copy(j).start()
        own = part_ref[pl.ds(pl.multiple_of(me.g * 8, 8), 8), :]
        for s in range(1, 16):
            a_copy(me.g, s, owner_of((me.g + 16 - s) % 16)).wait_recv()
            own += first[s]
        mine[...] = own
        second[me.h] = own

        @pl.loop(1, 32)
        def _(s):
            push(mine, second.at[me.h], b_send.at[s], b_recv.at[me.h], over_tok(s)).start()

    for h in range(8):
        source = (me.g, h * 4 + me.owner_q)

        @pl.when(source[1] != me.t)
        def _():
            push(mine, second.at[h], b_send.at[0], b_recv.at[h], source).wait_recv()

    total = second[0]
    for h in range(1, 8):
        total += second[h]
    rows[...] = total
    here = pl.ds(pl.multiple_of(me.g * 8, 8), 8)
    total_ref[here, :] = total
    for s in range(1, 16):
        push(rows, total_ref.at[here], c_send.at[s], c_recv.at[s], over_grp(s)).start()
    for s in range(1, 16):
        there = pl.ds(pl.multiple_of(((me.g + 16 - s) % 16) * 8, 8), 8)
        push(rows, total_ref.at[there], c_send.at[s], c_recv.at[s], over_grp(16 - s)).wait_recv()
    for s in range(1, 16):
        push(rows, total_ref.at[here], c_send.at[s], c_recv.at[s], over_grp(s)).wait_send()

    @pl.when(is_owner)
    def _():
        out_ref[...] = feat_ref[pl.ds(pl.multiple_of(me.q * 256, 256), 256), :]
        for s in range(1, 16):
            g = (me.g + s) % 16
            a_copy(g, s, owner_of(g)).wait_send()

        @pl.loop(1, 32)
        def _(s):
            push(mine, second.at[me.h], b_send.at[s], b_recv.at[me.h], over_tok(s)).wait_send()

        for j in range(1, 4):
            feature_copy(j).wait_send()

    @pl.when(jnp.logical_not(is_owner))
    def _():
        push(feat_ref.at[pl.ds(0, 256), :], out_ref, f_send.at[0], f_recv, (me.g, me.owner)).wait_recv()


def finish(partial, features):
    dma = pltpu.SemaphoreType.DMA
    return pl.pallas_call(
        reduce_kernel,
        out_shape=(
            jax.ShapeDtypeStruct((128, 128), F32),
            jax.ShapeDtypeStruct((256, 2048), BF16),
        ),
        in_specs=[VM, VM],
        out_specs=(VM, VM),
        scratch_shapes=[
            pltpu.VMEM((16, 8, 128), F32),
            pltpu.VMEM((8, 128), F32),
            pltpu.VMEM((8, 8, 128), F32),
            pltpu.VMEM((8, 128), F32),
            dma((4,)), dma, dma((16,)), dma((16,)), dma((32,)), dma((8,)), dma((16,)), dma((16,)),
        ],
        compiler_params=pltpu.CompilerParams(collective_id=2, has_side_effects=True),
        name="finish",
    )(partial, features)


def centered_blocks(feats):
    wide = feats.astype(F32)
    mean = jnp.sum(wide, axis=0) / 1024
    projection = jnp.sum(wide * mean, axis=1)
    mean_square = jnp.sum(mean * mean)
    pieces = [feats[256 * i : 256 * i + 256] for i in range(4)]
    parts = [projection[256 * i : 256 * i + 256] for i in range(4)]
    diagonal, upper = [], []
    for i in range(4):
        right = feats[256 * i :]
        gram = lax.dot_general(pieces[i], right, NT, preferred_element_type=F32)
        block = gram - parts[i][:, None] - projection[256 * i :][None, :] + mean_square
        block = block.astype(BF16)
        diagonal.append(block[:, :256])
        if i < 3:
            upper.append(block[:, 256:])
    return jnp.concatenate(diagonal + upper, axis=1)


def shards(probe_states, norm_gain, gate_weight, up_weight, down_weight, route_weight):
    feats = make_features(probe_states, norm_gain, gate_weight, up_weight, down_weight, route_weight)
    arrived = exchange(centered_blocks(feats))
    column = (lax.axis_index("tok") // 4 % 4) * 640 + lax.broadcasted_iota(jnp.int32, (1, 1, 1, 640), 3)
    weight = jnp.where(column < 1024, 1.0, 2.0).astype(BF16)
    left = (arrived * weight).reshape(128, -1)
    partial = lax.dot_general(left, arrived.reshape(128, -1), NT, preferred_element_type=F32)
    pair_totals, features = finish(partial, feats)
    diagonal = jnp.diagonal(pair_totals)
    cka = pair_totals / jnp.sqrt(diagonal[:, None] * diagonal[None, :])
    return (features, cka)


def solution(mesh):
    return jax.shard_map(
        shards,
        mesh=mesh,
        in_specs=(
            P("tok", None),
            P(),
            P(("grp", "tok"), None),
            P(("grp", "tok"), None),
            P(("grp", "tok"), None),
            P(("grp", "tok"), None),
        ),
        out_specs=(P(("grp", "tok"), None), P()),
        check_vma=False,
    )
```

```python
import functools

import jax
import jax.numpy as jnp
from jax import lax
from jax.experimental import pallas as pl
from jax.experimental.pallas import tpu as pltpu
from jax.sharding import PartitionSpec as P

F32 = jnp.float32
BF16 = jnp.bfloat16
NT = (((1,), (1,)), ((), ()))
MESH = pl.DeviceIdType.MESH
VM = pl.BlockSpec(memory_space=pltpu.VMEM)


class Place:
    def __init__(self):
        self.g = lax.axis_index("grp")
        self.t = lax.axis_index("tok")
        self.xl = self.g // 8
        self.y = (self.g // 2) % 4
        self.c = self.g % 2
        self.xh = self.t // 16
        self.z = self.t % 16
        self.q = self.t % 4
        self.h = self.t // 4
        self.base = self.h * 4
        self.owner_q = 1 + self.c
        self.owner = self.base + self.owner_q
        self.rank = (self.q + 4 - self.owner_q) % 4

    def at_y(self, step):
        return (self.xl * 8 + ((self.y + step) % 4) * 2 + self.c, self.t)

    def at_x(self, step):
        x = (self.xh * 2 + self.xl + step) % 4
        return ((x % 2) * 8 + self.y * 2 + self.c, (x // 2) * 16 + self.z)

    def at_z(self, step):
        return (self.g, self.xh * 16 + (self.z + step) % 16)

    def at_core(self):
        return (self.xl * 8 + self.y * 2 + 1 - self.c, self.t)


def push(src, dst, send, recv, device):
    return pltpu.make_async_remote_copy(
        src_ref=src, dst_ref=dst, send_sem=send, recv_sem=recv, device_id=device, device_id_type=MESH
    )


def greet(devices):
    barrier = pltpu.get_barrier_semaphore()
    for device in devices:
        pl.semaphore_signal(barrier, inc=1, device_id=device, device_id_type=MESH)
    return barrier


def cka_kernel(
    x_hbm, gain_ref, gate_hbm, up_hbm, down_hbm, route_ref,
    out_ref, cka_ref,
    x_ref, gate_ref, up_ref, down_ref, wide_route, nrm, tok, hid, downs, routes,
    feats, column_sum, proj_column, proj_row, cen, mid, arr, folded, part, first, mine, second, rows_sum, total_ref,
    l_sem, z_send, z_recv, y_send, y_recv, x_send, x_recv, c_send, c_recv, w_send, w_recv, d_send, d_recv,
    f_send, f_recv, a_send, a_recv, b_send, b_recv, k_sem, p_send, p_recv, s_send, s_recv, t_send, t_recv,
):
    me = Place()
    is_owner = me.rank == 0
    not_owner = jnp.logical_not(is_owner)

    loads = [
        pltpu.make_async_copy(src, dst, l_sem.at[i])
        for i, (src, dst) in enumerate(
            ((x_hbm, x_ref), (down_hbm, down_ref), (gate_hbm, gate_ref), (up_hbm, up_ref))
        )
    ]
    for load in loads:
        load.start()

    def over_tok(step):
        return (me.g, (me.t + step) % 32)

    def over_grp(step):
        return ((me.g + step) % 16, me.t)

    def owner_in_grp(step):
        g = (me.g + step) % 16
        return g, (g, me.base + 1 + g % 2)

    def owner_in_tok(step):
        h = (me.h + step) % 8
        return h, (me.g, h * 4 + me.owner_q)

    partners = [over_tok(s) for s in range(1, 32)] + [over_grp(s) for s in range(1, 16)]
    partners += [me.at_x(3 - 2 * me.xl)]
    barrier = greet(partners)

    @pl.when(is_owner)
    def _():
        for s in range(1, 16, 2):
            pl.semaphore_signal(barrier, inc=1, device_id=owner_in_grp(s)[1], device_id_type=MESH)

    loads[0].wait()
    states = x_ref[...].astype(F32)
    scale = lax.rsqrt(jnp.mean(states * states, axis=1, keepdims=True) + 1e-06)
    nrm[...] = (states * scale * gain_ref[...]).astype(BF16)
    wide_route[...] = jnp.broadcast_to(route_ref[...], (8, 256))
    group = me.c * 8 + me.xl * 4 + me.y
    rows = pl.ds(pl.multiple_of(me.t * 32, 32), 32)
    columns = pl.ds(pl.multiple_of(group * 128, 128), 128)
    tok[rows, columns] = nrm[:, columns]
    loads[1].wait()

    @pl.when(is_owner)
    def _():
        pl.semaphore_wait(barrier, len(partners) + 8)

    @pl.when(not_owner)
    def _():
        pl.semaphore_wait(barrier, len(partners))

    sends = []

    def start(copy):
        copy.start()
        sends.append(copy)

    for s in range(1, 16):
        start(push(nrm.at[:, columns], tok.at[rows, columns], z_send.at[s], z_recv.at[s], me.at_z(s)))
    for s in range(1, 16):
        source = pl.ds(pl.multiple_of((me.xh * 16 + (me.z + 16 - s) % 16) * 32, 32), 32)
        push(nrm.at[:, columns], tok.at[source, columns], z_send.at[s], z_recv.at[s], me.at_z(s)).wait_recv()

    def spot(step_x, y):
        x = (me.xh * 2 + me.xl + step_x) % 4
        row = pl.multiple_of((x // 2) * 512, 512)
        return row, pl.multiple_of((me.c * 8 + (x % 2) * 4 + y) * 128, 128)

    def y_copy(part, direction, source_step, slot):
        row, col = spot(0, (me.y + source_step) % 4)
        start_row, count = ((0, 512), (0, 256), (256, 256))[part]
        block = tok.at[pl.ds(row + start_row, count), pl.ds(col, 128)]
        return push(block, block, y_send.at[slot], y_recv.at[slot], me.at_y(direction))

    def x_copy(slot, direction, source_step, y):
        row, col = spot(source_step, y)
        block = tok.at[pl.ds(row, 512), pl.ds(col, 128)]
        return push(block, block, x_send.at[slot, y], x_recv.at[slot, y], me.at_x(direction))

    def core_copy(step_x, core):
        x = (me.xh * 2 + me.xl + step_x) % 4
        row = pl.multiple_of((x // 2) * 512, 512)
        col = pl.multiple_of((core * 8 + (x % 2) * 4) * 128, 128)
        block = tok.at[pl.ds(row, 512), pl.ds(col, 512)]
        return push(block, block, c_send.at[step_x], c_recv.at[step_x], me.at_core())

    start(y_copy(0, 1, 0, 0))
    start(y_copy(0, 3, 0, 1))
    start(x_copy(0, 1, 0, me.y))
    start(x_copy(1, 3, 0, me.y))

    owner = (me.g, me.owner)
    slot = (me.rank + 3) % 4
    down_copy = push(down_ref, downs.at[slot], w_send.at[0], w_recv.at[slot, 0], owner)
    route_copy = push(wide_route, routes.at[me.q], w_send.at[1], w_recv.at[slot, 1], owner)

    @pl.when(not_owner)
    def _():
        down_copy.start()
        route_copy.start()

    y_copy(0, 1, 3, 0).wait_recv()
    start(y_copy(1, 1, 3, 2))
    start(x_copy(0, 1, 0, (me.y + 3) % 4))
    start(x_copy(1, 3, 0, (me.y + 3) % 4))
    y_copy(0, 3, 1, 1).wait_recv()
    start(y_copy(2, 3, 1, 3))
    start(x_copy(0, 1, 0, (me.y + 1) % 4))
    start(x_copy(1, 3, 0, (me.y + 1) % 4))
    y_copy(1, 1, 2, 2).wait_recv()
    y_copy(2, 3, 2, 3).wait_recv()
    start(x_copy(0, 1, 0, (me.y + 2) % 4))
    start(x_copy(1, 3, 0, (me.y + 2) % 4))
    start(core_copy(0, me.c))

    for d in (0, 3, 1, 2):
        y = (me.y + d) % 4
        x_copy(0, 1, 3, y).wait_recv()
        x_copy(1, 3, 1, y).wait_recv()
        source = 3 - 2 * (y // 2)
        start(x_copy(2, 4 - source, source, y))
    start(core_copy(1, me.c))
    start(core_copy(3, me.c))

    def chunk_rows(k):
        block = (me.xh * 2 + k) % 4
        return block, pl.ds(pl.multiple_of(block * 256, 256), 256)

    def hidden_copy(k, source_slot):
        _, rows_k = chunk_rows(k)
        return push(
            hid.at[0, rows_k], hid.at[source_slot, rows_k], d_send.at[k], d_recv.at[source_slot, k], owner
        )

    def make_hidden(k):
        _, rows_k = chunk_rows(k)
        block = tok[rows_k, :]
        gate = lax.dot_general(block, gate_ref[...], NT, preferred_element_type=F32)
        upward = lax.dot_general(block, up_ref[...], NT, preferred_element_type=F32)
        hid[0, rows_k, :] = (gate / (1.0 + jnp.exp(-gate)) * upward).astype(BF16)

        @pl.when(not_owner)
        def _():
            hidden_copy(k, me.rank).start()

    loads[2].wait()
    loads[3].wait()
    core_copy(0, 1 - me.c).wait_recv()
    core_copy(1 + 2 * me.xl, 1 - me.c).wait_recv()

    @pl.loop(0, 2)
    def _(k):
        make_hidden(k)

    for d in (0, 3, 1, 2):
        y = (me.y + d) % 4
        x_copy(2, 1, 2, y).wait_recv()
    start(core_copy(2, me.c))
    core_copy(3 - 2 * me.xl, 1 - me.c).wait_recv()
    core_copy(2, 1 - me.c).wait_recv()

    @pl.loop(2, 4)
    def _(k):
        make_hidden(k)

    def feature_copy(k):
        block, rows_k = chunk_rows(k)
        return block, push(feats.at[rows_k, :], out_ref, f_send.at[k], f_recv, (me.g, me.base + block))

    def ship(k):
        block, copy = feature_copy(k)

        @pl.when(block != me.q)
        def _():
            copy.start()

    def first_copy(g_to, g_from, step, device):
        src = cen.at[pl.ds(pl.multiple_of(g_to * 16, 16), 16), :]
        return push(src, mid.at[g_from], a_send.at[step], a_recv.at[step], device)

    def slot_of(h):
        return (
            pl.ds(pl.multiple_of((h // 4) * 8, 8), 8),
            pl.ds(pl.multiple_of((h % 4) * 640, 128), 640),
        )

    def landing(g, h):
        return arr.at[pl.ds(pl.multiple_of((g * 8 + h) * 8, 8), 8), :]

    def many(step, device):
        block = arr.at[pl.ds(0, 128), :]
        return push(block, block, b_send.at[step], b_recv.at[step], device)

    def send_on(g):
        for s in range(1, 8):
            h, device = owner_in_tok(s)
            r, k = slot_of(h)
            push(mid.at[g, r, k], landing(g, me.h), b_send.at[s], b_recv.at[s], device).start()
        r, k = slot_of(me.h)
        pltpu.make_async_copy(mid.at[g, r, k], landing(g, me.h), k_sem).start()

    def part_copy(step):
        g, device = owner_in_grp(step)
        src = part.at[pl.ds(pl.multiple_of(g * 8, 8), 8), :]
        return push(src, first.at[step], p_send.at[step], p_recv.at[step], device)

    def row_copy(step):
        return push(mine, second.at[me.h], s_send.at[step], s_recv.at[me.h], over_tok(step))

    @pl.when(is_owner)
    def _():
        for j in range(1, 4):
            device = (me.g, me.base + (me.owner_q + j) % 4)
            push(down_ref, downs.at[j - 1], w_send.at[0], w_recv.at[j - 1, 0], device).wait_recv()
            push(
                wide_route, routes.at[(me.owner_q + j) % 4], w_send.at[1], w_recv.at[j - 1, 1], device
            ).wait_recv()
        routes[me.q] = wide_route[...]
        column_sum[...] = jnp.zeros_like(column_sum)

        @pl.loop(0, 4)
        def _(k):
            block, rows_k = chunk_rows(k)
            for j in range(1, 4):
                hidden_copy(k, j).wait_recv()

            @pl.when(k > 0)
            def _():
                ship(k - 1)

            route = routes[block]
            route_column = jnp.transpose(jnp.concatenate([route] * 16, axis=0))

            @pl.loop(0, 4)
            def _(n):
                cols = pl.ds(pl.multiple_of(n * 512, 512), 512)
                out = jnp.dot(hid[0, rows_k, :], down_ref[:, cols], preferred_element_type=F32)
                for j in range(1, 4):
                    out += jnp.dot(hid[j, rows_k, :], downs[j - 1, :, cols], preferred_element_type=F32)
                wide = jnp.concatenate([route_column] * 4, axis=1)
                rounded = (out * wide).astype(BF16)
                feats[rows_k, cols] = rounded
                column_sum[:, cols] += jnp.sum(rounded.astype(F32).reshape(32, 8, 512), axis=0)

        mean = jnp.sum(column_sum[...], axis=0, keepdims=True) / 1024
        mean_square = jnp.sum(mean * mean, axis=1, keepdims=True)
        column_sum[...] = jnp.broadcast_to(mean, (8, 2048))

        @pl.loop(0, 4)
        def _(i):
            rows_i = pl.ds(pl.multiple_of(i * 256, 256), 256)
            total = jnp.zeros((256, 128), F32)
            for n in range(16):
                lanes = slice(n * 128, n * 128 + 128)
                total += feats[rows_i, lanes].astype(F32) * column_sum[0:1, lanes]
            projection = jnp.broadcast_to(jnp.sum(total, axis=1, keepdims=True), (256, 128))
            proj_column[rows_i, :] = projection
            proj_row[:, rows_i] = jnp.transpose(projection)[0:8, :]

        ship(3)

        @pl.loop(0, 10)
        def _(p):
            i = p % 4
            j = (i + p // 4) % 4
            rows_i = pl.ds(pl.multiple_of(i * 256, 256), 256)
            rows_j = pl.ds(pl.multiple_of(j * 256, 256), 256)
            gram = lax.dot_general(feats[rows_i, :], feats[rows_j, :], NT, preferred_element_type=F32)
            column = proj_column[rows_i, :]
            block = gram - jnp.concatenate([column, column], axis=1) - proj_row[0:1, rows_j] + mean_square
            cen[:, pl.ds(pl.multiple_of(p * 256, 256), 256)] = block.astype(BF16)

        mid[me.g] = cen[pl.ds(pl.multiple_of(me.g * 16, 16), 16), :]
        for s in range(1, 16):
            g, device = owner_in_grp(s)
            first_copy(g, me.g, s, device).start()
        send_on(me.g)

        @pl.loop(1, 16)
        def _(s):
            g, device = owner_in_grp(16 - s)
            first_copy(me.g, g, s, device).wait_recv()
            send_on(g)

        whole = arr.at[pl.ds(0, 128), :]
        pltpu.make_async_copy(whole, whole, k_sem).wait()
        for s in range(1, 8):
            many(s, owner_in_tok(s)[1]).wait_recv()

        position = (me.h % 4) * 640 + lax.broadcasted_iota(jnp.int32, (1, 640), 1)
        weight = jnp.where(position < 1024, 1.0, 2.0)
        lane = lax.broadcasted_iota(jnp.int32, (256, 256), 1) % 8
        sublane = lax.broadcasted_iota(jnp.int32, (256, 256), 0) % 8

        @pl.loop(0, 4)
        def _(i):
            rows_i = pl.ds(pl.multiple_of(i * 256, 256), 256)
            left = (arr[rows_i, :].astype(F32) * weight).astype(BF16)

            @pl.loop(0, 4)
            def _(j):
                rows_j = pl.ds(pl.multiple_of(j * 256, 256), 256)
                block = lax.dot_general(left, arr[rows_j, :], NT, preferred_element_type=F32)
                block = jnp.where(lane == sublane, block, 0.0)
                folded[pl.ds(pl.multiple_of(i * 32, 32), 32), rows_j] = jnp.sum(block.reshape(32, 8, 256), axis=1)

        pick = lax.broadcasted_iota(jnp.int32, (1024, 128), 0) // 8
        pick = (pick == lax.broadcasted_iota(jnp.int32, (1024, 128), 1)).astype(F32).astype(BF16)
        rest = folded[...]
        result = jnp.zeros((128, 128), F32)
        for _ in range(3):
            top = rest.astype(BF16)
            rest = rest - top.astype(F32)
            result += jnp.dot(top, pick, preferred_element_type=F32)
        part[...] = result

        for s in range(1, 16):
            part_copy(s).start()
        own = part[pl.ds(pl.multiple_of(me.g * 8, 8), 8), :]
        for s in range(1, 16):
            part_copy(s).wait_recv()
            own += first[s]
        mine[...] = own
        second[me.h] = own

        @pl.loop(1, 32)
        def _(s):
            row_copy(s).start()

    for h in range(8):
        source = (me.g, h * 4 + me.owner_q)

        @pl.when(source[1] != me.t)
        def _():
            push(mine, second.at[h], s_send.at[0], s_recv.at[h], source).wait_recv()

    total = second[0]
    for h in range(1, 8):
        total += second[h]
    rows_sum[...] = total

    def total_copy(step, source):
        there = pl.ds(pl.multiple_of(source * 8, 8), 8)
        return push(rows_sum, total_ref.at[there], t_send.at[step], t_recv.at[step], over_grp(step))

    total_ref[pl.ds(pl.multiple_of(me.g * 8, 8), 8), :] = total
    for s in range(1, 16):
        total_copy(s, me.g).start()
    for s in range(1, 16):
        total_copy(s, (me.g + 16 - s) % 16).wait_recv()

    pairs = total_ref[...]
    eye = lax.broadcasted_iota(jnp.int32, (128, 128), 0) == lax.broadcasted_iota(jnp.int32, (128, 128), 1)
    only = jnp.where(eye, pairs, 0.0)
    down = jnp.sum(only, axis=1, keepdims=True)
    across = jnp.sum(only, axis=0, keepdims=True)
    cka_ref[...] = pairs / jnp.sqrt(down * across)

    for s in range(1, 16):
        total_copy(s, me.g).wait_send()

    @pl.when(is_owner)
    def _():
        out_ref[...] = feats[pl.ds(pl.multiple_of(me.q * 256, 256), 256), :]
        for s in range(1, 16):
            g, device = owner_in_grp(s)
            first_copy(g, me.g, s, device).wait_send()
            part_copy(s).wait_send()
        for s in range(1, 8):
            many(s, owner_in_tok(s)[1]).wait_send()

        @pl.loop(1, 32)
        def _(s):
            row_copy(s).wait_send()

        @pl.loop(0, 4)
        def _(k):
            block, copy = feature_copy(k)

            @pl.when(block != me.q)
            def _():
                copy.wait_send()

    @pl.when(not_owner)
    def _():
        down_copy.wait_send()
        route_copy.wait_send()

        @pl.loop(0, 4)
        def _(k):
            hidden_copy(k, me.rank).wait_send()

        push(feats.at[pl.ds(0, 256), :], out_ref, f_send.at[0], f_recv, owner).wait_recv()

    for copy in sends:
        copy.wait_send()


def shards(probe_states, norm_gain, gate_weight, up_weight, down_weight, route_weight):
    dma = pltpu.SemaphoreType.DMA
    hbm = pl.BlockSpec(memory_space=pl.ANY)
    return pl.pallas_call(
        cka_kernel,
        out_shape=(
            jax.ShapeDtypeStruct((256, 2048), BF16),
            jax.ShapeDtypeStruct((128, 128), F32),
        ),
        in_specs=[hbm, VM, hbm, hbm, hbm, VM],
        out_specs=(VM, VM),
        scratch_shapes=[
            pltpu.VMEM((32, 2048), BF16),
            pltpu.VMEM((192, 2048), BF16),
            pltpu.VMEM((192, 2048), BF16),
            pltpu.VMEM((192, 2048), BF16),
            pltpu.VMEM((8, 256), F32),
            pltpu.VMEM((32, 2048), BF16),
            pltpu.VMEM((1024, 2048), BF16),
            pltpu.VMEM((4, 1024, 192), BF16),
            pltpu.VMEM((3, 192, 2048), BF16),
            pltpu.VMEM((4, 8, 256), F32),
            pltpu.VMEM((1024, 2048), BF16),
            pltpu.VMEM((8, 2048), F32),
            pltpu.VMEM((1024, 128), F32),
            pltpu.VMEM((8, 1024), F32),
            pltpu.VMEM((256, 2560), BF16),
            pltpu.VMEM((16, 16, 2560), BF16),
            pltpu.VMEM((1024, 640), BF16),
            pltpu.VMEM((128, 1024), F32),
            pltpu.VMEM((128, 128), F32),
            pltpu.VMEM((16, 8, 128), F32),
            pltpu.VMEM((8, 128), F32),
            pltpu.VMEM((8, 8, 128), F32),
            pltpu.VMEM((8, 128), F32),
            pltpu.VMEM((128, 128), F32),
            dma((4,)), dma((16,)), dma((16,)), dma((4,)), dma((4,)), dma((3, 4)), dma((3, 4)),
            dma((4,)), dma((4,)), dma((2,)), dma((3, 2)), dma((4,)), dma((4, 4)),
            dma((4,)), dma, dma((16,)), dma((16,)), dma((8,)), dma((8,)), dma,
            dma((16,)), dma((16,)), dma((32,)), dma((8,)), dma((16,)), dma((16,)),
        ],
        compiler_params=pltpu.CompilerParams(
            collective_id=0, has_side_effects=True, vmem_limit_bytes=56 << 20
        ),
        name="cka",
    )(probe_states, norm_gain[None, :], gate_weight, up_weight, down_weight, route_weight)


def solution(mesh):
    return jax.shard_map(
        shards,
        mesh=mesh,
        in_specs=(
            P("tok", None),
            P(),
            P(("grp", "tok"), None),
            P(("grp", "tok"), None),
            P(("grp", "tok"), None),
            P(("grp", "tok"), None),
        ),
        out_specs=(P(("grp", "tok"), None), P()),
        check_vma=False,
    )
```

```python
import functools

import jax
import jax.numpy as jnp
from jax import lax
from jax.experimental import pallas as pl
from jax.experimental.pallas import tpu as pltpu
from jax.sharding import PartitionSpec as P

CUTS = (0, 512, 1536, 2048)
F32 = jnp.float32
BF16 = jnp.bfloat16
NT = (((1,), (1,)), ((), ()))
MESH = pl.DeviceIdType.MESH
FAR_FIRST = sorted(range(1, 16), key=lambda s: -min(s, 16 - s))
TOK_FAR_FIRST = sorted(range(1, 32), key=lambda s: -min(s % 16, 16 - s % 16))
VM = pl.BlockSpec(memory_space=pltpu.VMEM)


class Place:
    def __init__(self):
        self.g = lax.axis_index("grp")
        self.t = lax.axis_index("tok")
        self.xl = self.g // 8
        self.y = (self.g // 2) % 4
        self.c = self.g % 2
        self.xh = self.t // 16
        self.z = self.t % 16
        self.q = self.t % 4
        self.h = self.t // 4
        self.base = self.h * 4
        self.owner_q = 1 + self.c
        self.owner = self.base + self.owner_q
        self.rank = (self.q + 4 - self.owner_q) % 4

    def at_y(self, step):
        return (self.xl * 8 + ((self.y + step) % 4) * 2 + self.c, self.t)

    def at_x(self, step):
        x = (self.xh * 2 + self.xl + step) % 4
        return ((x % 2) * 8 + self.y * 2 + self.c, (x // 2) * 16 + self.z)

    def at_z(self, step):
        return (self.g, self.xh * 16 + (self.z + step) % 16)

    def at_core(self):
        return (self.xl * 8 + self.y * 2 + 1 - self.c, self.t)


def push(src, dst, send, recv, device):
    return pltpu.make_async_remote_copy(
        src_ref=src, dst_ref=dst, send_sem=send, recv_sem=recv, device_id=device, device_id_type=MESH
    )


def greet(devices):
    barrier = pltpu.get_barrier_semaphore()
    for device in devices:
        pl.semaphore_signal(barrier, inc=1, device_id=device, device_id_type=MESH)
    return barrier


def cka_kernel(
    x_hbm, gain_ref, gate_hbm, up_hbm, down_hbm, route_ref,
    out_ref, cka_ref,
    x_ref, gate_ref, up_ref, down_ref, wide_route, nrm, tok, gate_sum, up_sum, hid, downs, routes,
    feats, column_sum, proj_column, proj_row, cen, mid, arr, folded, part, first, mine, second, rows_sum, total_ref,
    l_sem, z_send, z_recv, h_send, h_recv, y_send, y_recv, x_send, x_recv, c_send, c_recv, w_send, w_recv, d_send, d_recv,
    f_send, f_recv, a_send, a_recv, b_send, b_recv, k_sem, p_send, p_recv, s_send, s_recv, t_send, t_recv,
):
    me = Place()
    is_owner = me.rank == 0
    not_owner = jnp.logical_not(is_owner)

    loads = [
        pltpu.make_async_copy(src, dst, l_sem.at[i])
        for i, (src, dst) in enumerate(
            ((x_hbm, x_ref), (down_hbm, down_ref), (gate_hbm, gate_ref), (up_hbm, up_ref))
        )
    ]
    for load in loads:
        load.start()

    def over_tok(step):
        return (me.g, (me.t + step) % 32)

    def over_grp(step):
        return ((me.g + step) % 16, me.t)

    def owner_in_grp(step):
        g = (me.g + step) % 16
        return g, (g, me.base + 1 + g % 2)

    def owner_in_tok(step):
        h = (me.h + step) % 8
        return h, (me.g, h * 4 + me.owner_q)

    partners = [over_tok(s) for s in range(1, 32)] + [over_grp(s) for s in range(1, 16)]
    partners += [me.at_x(3 - 2 * me.xl)]
    barrier = greet(partners)

    @pl.when(is_owner)
    def _():
        for s in range(1, 16, 2):
            pl.semaphore_signal(barrier, inc=1, device_id=owner_in_grp(s)[1], device_id_type=MESH)

    loads[0].wait()
    states = x_ref[...].astype(F32)
    scale = lax.rsqrt(jnp.mean(states * states, axis=1, keepdims=True) + 1e-06)
    nrm[...] = (states * scale * gain_ref[...]).astype(BF16)
    wide_route[...] = jnp.broadcast_to(route_ref[...], (8, 256))
    group = me.c * 8 + me.xl * 4 + me.y
    rows = pl.ds(pl.multiple_of(me.t * 32, 32), 32)
    columns = pl.ds(pl.multiple_of(group * 128, 128), 128)
    tok[rows, columns] = nrm[:, columns]
    loads[1].wait()

    @pl.when(is_owner)
    def _():
        pl.semaphore_wait(barrier, len(partners) + 8)

    @pl.when(not_owner)
    def _():
        pl.semaphore_wait(barrier, len(partners))

    sends = []

    def start(copy):
        copy.start()
        sends.append(copy)

    for s in FAR_FIRST:
        start(push(nrm.at[:, columns], tok.at[rows, columns], z_send.at[s], z_recv.at[s], me.at_z(s)))
    for s in range(1, 16):
        source = pl.ds(pl.multiple_of((me.xh * 16 + (me.z + 16 - s) % 16) * 32, 32), 32)
        push(nrm.at[:, columns], tok.at[source, columns], z_send.at[s], z_recv.at[s], me.at_z(s)).wait_recv()

    def spot(step_x, y):
        x = (me.xh * 2 + me.xl + step_x) % 4
        row = pl.multiple_of((x // 2) * 512, 512)
        return row, pl.multiple_of((me.c * 8 + (x % 2) * 4 + y) * 128, 128)

    def y_copy(half, part, direction, source_step, slot):
        row, col = spot(2 * half, (me.y + source_step) % 4)
        start_row, count = ((0, 512), (0, 256), (256, 256))[part]
        block = tok.at[pl.ds(row + start_row, count), pl.ds(col, 128)]
        return push(block, block, y_send.at[half, slot], y_recv.at[half, slot], me.at_y(direction))

    def x_copy(slot, direction, source_step, y):
        row, col = spot(source_step, y)
        block = tok.at[pl.ds(row, 512), pl.ds(col, 128)]
        return push(block, block, x_send.at[slot, y], x_recv.at[slot, y], me.at_x(direction))

    def both_x(step_y):
        y = (me.y + step_y) % 4
        start(x_copy(0, 1, 0, y))
        start(x_copy(1, 3, 0, y))

    def core_block(step_x, core):
        x = (me.xh * 2 + me.xl + step_x) % 4
        row = pl.multiple_of((x // 2) * 512, 512)
        col = pl.multiple_of((core * 8 + (x % 2) * 4) * 128, 128)
        block = tok.at[pl.ds(row, 512), pl.ds(col, 512)]
        return push(block, block, c_send.at[step_x, 0], c_recv.at[step_x, 0], me.at_core())

    def core_piece(step_x, y, core):
        x = (me.xh * 2 + me.xl + step_x) % 4
        row = pl.multiple_of((x // 2) * 512, 512)
        col = pl.multiple_of((core * 8 + (x % 2) * 4 + y) * 128, 128)
        block = tok.at[pl.ds(row, 512), pl.ds(col, 128)]
        return push(block, block, c_send.at[step_x, y], c_recv.at[step_x, y], me.at_core())

    row, col = spot(0, me.y)
    own = tok.at[pl.ds(row, 512), pl.ds(col, 128)]
    start(push(own, own, h_send, h_recv, me.at_x(2)))
    start(y_copy(0, 0, 1, 0, 0))
    start(y_copy(0, 0, 3, 0, 1))
    both_x(0)

    owner = (me.g, me.owner)
    slot = (me.rank + 3) % 4
    down_copy = push(down_ref, downs.at[slot], w_send.at[0], w_recv.at[slot, 0], owner)
    route_copy = push(wide_route, routes.at[me.q], w_send.at[1], w_recv.at[slot, 1], owner)

    @pl.when(not_owner)
    def _():
        down_copy.start()
        route_copy.start()

    y_copy(0, 0, 1, 3, 0).wait_recv()
    start(y_copy(0, 1, 1, 3, 2))
    both_x(3)
    y_copy(0, 0, 3, 1, 1).wait_recv()
    start(y_copy(0, 2, 3, 1, 3))
    both_x(1)
    row, col = spot(2, me.y)
    other = tok.at[pl.ds(row, 512), pl.ds(col, 128)]
    push(other, other, h_send, h_recv, me.at_x(2)).wait_recv()
    start(y_copy(1, 0, 1, 0, 0))
    start(y_copy(1, 0, 3, 0, 1))
    y_copy(0, 1, 1, 2, 2).wait_recv()
    y_copy(0, 2, 3, 2, 3).wait_recv()
    both_x(2)
    start(core_block(0, me.c))
    y_copy(1, 0, 1, 3, 0).wait_recv()
    start(y_copy(1, 1, 1, 3, 2))
    y_copy(1, 0, 3, 1, 1).wait_recv()
    start(y_copy(1, 2, 3, 1, 3))
    y_copy(1, 1, 1, 2, 2).wait_recv()
    y_copy(1, 2, 3, 2, 3).wait_recv()
    start(core_block(2, me.c))

    def accumulate(step_x, core, first):
        x = (me.xh * 2 + me.xl + step_x) % 4
        cols = pl.ds(pl.multiple_of((core * 8 + (x % 2) * 4) * 128, 128), 512)

        @pl.loop(0, 2)
        def _(i):
            chunk = pl.ds(pl.multiple_of((x // 2) * 512 + i * 256, 256), 256)
            block = tok[chunk, cols]
            for weight_ref, sums in ((gate_ref, gate_sum), (up_ref, up_sum)):
                product = lax.dot_general(block, weight_ref[:, cols], NT, preferred_element_type=F32)
                sums[chunk, :] = product if first else sums[chunk, :] + product

    def chunk_rows(k):
        block = (me.xh * 2 + k) % 4
        return block, pl.ds(pl.multiple_of(block * 256, 256), 256)

    def hidden_copy(k, source_slot):
        _, rows_k = chunk_rows(k)
        return push(
            hid.at[0, rows_k], hid.at[source_slot, rows_k], d_send.at[k], d_recv.at[source_slot, k], owner
        )

    def make_hidden(k):
        _, rows_k = chunk_rows(k)
        gate = gate_sum[rows_k, :]
        hid[0, rows_k, :] = (gate / (1.0 + jnp.exp(-gate)) * up_sum[rows_k, :]).astype(BF16)

        @pl.when(not_owner)
        def _():
            hidden_copy(k, me.rank).start()

    def along_x(d):
        y = (me.y + d) % 4
        x_copy(0, 1, 3, y).wait_recv()
        start(core_piece(3, y, me.c))
        x_copy(1, 3, 1, y).wait_recv()
        start(core_piece(1, y, me.c))

    peer = 1 - me.c
    near, far = 1 + 2 * me.xl, 3 - 2 * me.xl
    loads[2].wait()
    loads[3].wait()
    accumulate(0, me.c, True)
    along_x(0)
    core_block(0, peer).wait_recv()
    accumulate(0, peer, False)
    along_x(3)
    accumulate(2, me.c, True)
    core_block(2, peer).wait_recv()
    along_x(1)
    accumulate(2, peer, False)
    along_x(2)
    accumulate(near, me.c, False)
    for d in (0, 3, 1, 2):
        core_piece(near, (me.y + d) % 4, peer).wait_recv()
    accumulate(near, peer, False)

    @pl.loop(0, 2)
    def _(k):
        make_hidden(k)

    accumulate(far, me.c, False)
    for d in (0, 3, 1, 2):
        core_piece(far, (me.y + d) % 4, peer).wait_recv()
    accumulate(far, peer, False)

    @pl.loop(2, 4)
    def _(k):
        make_hidden(k)

    def feature_copy(k, part):
        block, rows_k = chunk_rows(k)
        cols = slice(CUTS[part], CUTS[part + 1])
        device = (me.g, me.base + block)
        return block, push(feats.at[rows_k, cols], out_ref.at[:, cols], f_send.at[part, k], f_recv, device)

    def ship(k, part):
        block, copy = feature_copy(k, part)

        @pl.when(block != me.q)
        def _():
            copy.start()

    def first_copy(batch, g_to, g_from, step, device):
        cols = slice(1280 * batch, 1280 * batch + 1280)
        src = cen.at[pl.ds(pl.multiple_of(g_to * 16, 16), 16), cols]
        return push(src, mid.at[g_from, :, cols], a_send.at[batch, step], a_recv.at[batch, step], device)

    def first_step(batch):
        cols = slice(1280 * batch, 1280 * batch + 1280)
        mid[me.g, :, cols] = cen[pl.ds(pl.multiple_of(me.g * 16, 16), 16), cols]
        for s in range(1, 16):
            g, device = owner_in_grp(s)
            first_copy(batch, g, me.g, s, device).start()

    def slot_of(h):
        return (
            pl.ds(pl.multiple_of((h // 4) * 8, 8), 8),
            pl.ds(pl.multiple_of((h % 4) * 640, 128), 640),
        )

    def landing(g, h):
        return arr.at[pl.ds(pl.multiple_of((g * 8 + h) * 8, 8), 8), :]

    def many(step, device):
        block = arr.at[pl.ds(0, 128), :]
        return push(block, block, b_send.at[step], b_recv.at[step], device)

    def send_on(batch, g):
        for s in (2, 6, 1, 3, 5, 7, 4):
            h, device = owner_in_tok(s)
            r, k = slot_of(h)

            @pl.when((h % 4) // 2 == batch)
            def _():
                push(mid.at[g, r, k], landing(g, me.h), b_send.at[s], b_recv.at[s], device).start()

        r, k = slot_of(me.h)

        @pl.when((me.h % 4) // 2 == batch)
        def _():
            pltpu.make_async_copy(mid.at[g, r, k], landing(g, me.h), k_sem).start()

    def part_copy(step):
        g, device = owner_in_grp(step)
        src = part.at[pl.ds(pl.multiple_of(g * 8, 8), 8), :]
        return push(src, first.at[step], p_send.at[step], p_recv.at[step], device)

    def row_copy(step):
        return push(mine, second.at[me.h], s_send.at[step], s_recv.at[me.h], over_tok(step))

    @pl.when(is_owner)
    def _():
        for j in range(1, 4):
            device = (me.g, me.base + (me.owner_q + j) % 4)
            push(down_ref, downs.at[j - 1], w_send.at[0], w_recv.at[j - 1, 0], device).wait_recv()
            push(
                wide_route, routes.at[(me.owner_q + j) % 4], w_send.at[1], w_recv.at[j - 1, 1], device
            ).wait_recv()
        routes[me.q] = wide_route[...]
        column_sum[...] = jnp.zeros_like(column_sum)

        @pl.loop(0, 4)
        def _(k):
            block, rows_k = chunk_rows(k)
            for j in range(1, 4):
                hidden_copy(k, j).wait_recv()

            route = routes[block]
            route_column = jnp.transpose(jnp.concatenate([route] * 16, axis=0))

            @pl.loop(0, 4)
            def _(n):
                cols = pl.ds(pl.multiple_of(n * 512, 512), 512)
                out = jnp.dot(hid[0, rows_k, :], down_ref[:, cols], preferred_element_type=F32)
                for j in range(1, 4):
                    out += jnp.dot(hid[j, rows_k, :], downs[j - 1, :, cols], preferred_element_type=F32)
                wide = jnp.concatenate([route_column] * 4, axis=1)
                rounded = (out * wide).astype(BF16)
                feats[rows_k, cols] = rounded
                column_sum[:, cols] += jnp.sum(rounded.astype(F32).reshape(32, 8, 512), axis=0)

        for k in range(3):
            ship(k, 0)
        mean = jnp.sum(column_sum[...], axis=0, keepdims=True) / 1024
        mean_square = jnp.sum(mean * mean, axis=1, keepdims=True)
        column_sum[...] = jnp.broadcast_to(mean, (8, 2048))

        @pl.loop(0, 4)
        def _(i):
            rows_i = pl.ds(pl.multiple_of(i * 256, 256), 256)
            total = jnp.zeros((256, 128), F32)
            for n in range(16):
                lanes = slice(n * 128, n * 128 + 128)
                total += feats[rows_i, lanes].astype(F32) * column_sum[0:1, lanes]
            projection = jnp.broadcast_to(jnp.sum(total, axis=1, keepdims=True), (256, 128))
            proj_column[rows_i, :] = projection
            proj_row[:, rows_i] = jnp.transpose(projection)[0:8, :]

        ship(3, 0)

        def gram_block(p):
            i = p % 4
            j = (i + p // 4) % 4
            rows_i = pl.ds(pl.multiple_of(i * 256, 256), 256)
            rows_j = pl.ds(pl.multiple_of(j * 256, 256), 256)
            gram = lax.dot_general(feats[rows_i, :], feats[rows_j, :], NT, preferred_element_type=F32)
            column = proj_column[rows_i, :]
            block = gram - jnp.concatenate([column, column], axis=1) - proj_row[0:1, rows_j] + mean_square
            cen[:, pl.ds(pl.multiple_of(p * 256, 256), 256)] = block.astype(BF16)

        for batch in (0, 1):
            pl.loop(5 * batch, 5 * batch + 5)(gram_block)
            first_step(batch)

        for batch in (0, 1):
            send_on(batch, me.g)

            @pl.loop(1, 16)
            def _(s):
                g, device = owner_in_grp(16 - s)
                first_copy(batch, me.g, g, s, device).wait_recv()
                send_on(batch, g)

        out_ref[...] = feats[pl.ds(pl.multiple_of(me.q * 256, 256), 256), :]
        whole = arr.at[pl.ds(0, 128), :]
        pltpu.make_async_copy(whole, whole, k_sem).wait()
        for s in range(1, 8):
            many(s, owner_in_tok(s)[1]).wait_recv()

        position = (me.h % 4) * 640 + lax.broadcasted_iota(jnp.int32, (1, 640), 1)
        weight = jnp.where(position < 1024, 1.0, 2.0)
        lane = lax.broadcasted_iota(jnp.int32, (256, 256), 1) % 8
        sublane = lax.broadcasted_iota(jnp.int32, (256, 256), 0) % 8

        pick = lax.broadcasted_iota(jnp.int32, (1024, 128), 0) // 8
        pick = (pick == lax.broadcasted_iota(jnp.int32, (1024, 128), 1)).astype(F32).astype(BF16)
        folded[...] = jnp.zeros_like(folded)
        for k in range(4):
            ship(k, 1)
        for i in range(4):
            left = (arr[256 * i : 256 * i + 256, :].astype(F32) * weight).astype(BF16)

            @pl.loop(i, 4)
            def _(j):
                rows_j = pl.ds(pl.multiple_of(j * 256, 256), 256)
                block = lax.dot_general(left, arr[rows_j, :], NT, preferred_element_type=F32)
                block = jnp.where(lane == sublane, block, 0.0)
                folded[32 * i : 32 * i + 32, rows_j] = jnp.sum(block.reshape(32, 8, 256), axis=1)

            rest = folded[32 * i : 32 * i + 32, :]
            result = jnp.zeros((32, 128), F32)
            for _ in range(3):
                top = rest.astype(BF16)
                rest = rest - top.astype(F32)
                result += jnp.dot(top, pick, preferred_element_type=F32)
            part[32 * i : 32 * i + 32, :] = result
            for g in range(4 * i, 4 * i + 4):

                @pl.when(me.g != g)
                def _():
                    part_copy((g + 16 - me.g) % 16).start()

        own = part[pl.ds(pl.multiple_of(me.g * 8, 8), 8), :]
        for s in range(1, 16):
            part_copy(s).wait_recv()
            own += first[s]
        mine[...] = own
        second[me.h] = own

        for s in TOK_FAR_FIRST:
            row_copy(s).start()
        for k in range(4):
            ship(k, 2)

    for h in range(8):
        source = (me.g, h * 4 + me.owner_q)

        @pl.when(source[1] != me.t)
        def _():
            push(mine, second.at[h], s_send.at[0], s_recv.at[h], source).wait_recv()

    total = second[0]
    for h in range(1, 8):
        total += second[h]
    rows_sum[...] = total

    def total_copy(step, source):
        there = pl.ds(pl.multiple_of(source * 8, 8), 8)
        return push(rows_sum, total_ref.at[there], t_send.at[step], t_recv.at[step], over_grp(step))

    total_ref[pl.ds(pl.multiple_of(me.g * 8, 8), 8), :] = total
    for s in range(1, 16):
        total_copy(s, me.g).start()
    for s in range(1, 16):
        total_copy(s, (me.g + 16 - s) % 16).wait_recv()

    pairs = total_ref[...]
    row = lax.broadcasted_iota(jnp.int32, (128, 128), 0)
    col = lax.broadcasted_iota(jnp.int32, (128, 128), 1)
    pairs = jnp.where(row // 32 <= col // 32, pairs, jnp.transpose(pairs))
    eye = row == col
    only = jnp.where(eye, pairs, 0.0)
    down = jnp.sum(only, axis=1, keepdims=True)
    across = jnp.sum(only, axis=0, keepdims=True)
    cka_ref[...] = pairs / jnp.sqrt(down * across)

    for s in range(1, 16):
        total_copy(s, me.g).wait_send()

    @pl.when(is_owner)
    def _():
        for s in range(1, 16):
            g, device = owner_in_grp(s)
            for batch in (0, 1):
                first_copy(batch, g, me.g, s, device).wait_send()
            part_copy(s).wait_send()
        for s in range(1, 8):
            many(s, owner_in_tok(s)[1]).wait_send()

        @pl.loop(1, 32)
        def _(s):
            row_copy(s).wait_send()

        for k in range(4):
            for part in range(3):
                block, copy = feature_copy(k, part)

                @pl.when(block != me.q)
                def _():
                    copy.wait_send()

    @pl.when(not_owner)
    def _():
        down_copy.wait_send()
        route_copy.wait_send()

        @pl.loop(0, 4)
        def _(k):
            hidden_copy(k, me.rank).wait_send()

        push(feats.at[pl.ds(0, 256), :], out_ref, f_send.at[0, 0], f_recv, owner).wait_recv()

    for copy in sends:
        copy.wait_send()


def shards(probe_states, norm_gain, gate_weight, up_weight, down_weight, route_weight):
    dma = pltpu.SemaphoreType.DMA
    hbm = pl.BlockSpec(memory_space=pl.ANY)
    return pl.pallas_call(
        cka_kernel,
        out_shape=(
            jax.ShapeDtypeStruct((256, 2048), BF16),
            jax.ShapeDtypeStruct((128, 128), F32),
        ),
        in_specs=[hbm, VM, hbm, hbm, hbm, VM],
        out_specs=(VM, VM),
        scratch_shapes=[
            pltpu.VMEM((32, 2048), BF16),
            pltpu.VMEM((192, 2048), BF16),
            pltpu.VMEM((192, 2048), BF16),
            pltpu.VMEM((192, 2048), BF16),
            pltpu.VMEM((8, 256), F32),
            pltpu.VMEM((32, 2048), BF16),
            pltpu.VMEM((1024, 2048), BF16),
            pltpu.VMEM((1024, 192), F32),
            pltpu.VMEM((1024, 192), F32),
            pltpu.VMEM((4, 1024, 192), BF16),
            pltpu.VMEM((3, 192, 2048), BF16),
            pltpu.VMEM((4, 8, 256), F32),
            pltpu.VMEM((1024, 2048), BF16),
            pltpu.VMEM((8, 2048), F32),
            pltpu.VMEM((1024, 128), F32),
            pltpu.VMEM((8, 1024), F32),
            pltpu.VMEM((256, 2560), BF16),
            pltpu.VMEM((16, 16, 2560), BF16),
            pltpu.VMEM((1024, 640), BF16),
            pltpu.VMEM((128, 1024), F32),
            pltpu.VMEM((128, 128), F32),
            pltpu.VMEM((16, 8, 128), F32),
            pltpu.VMEM((8, 128), F32),
            pltpu.VMEM((8, 8, 128), F32),
            pltpu.VMEM((8, 128), F32),
            pltpu.VMEM((128, 128), F32),
            dma((4,)), dma((16,)), dma((16,)), dma, dma, dma((2, 4)), dma((2, 4)), dma((2, 4)), dma((2, 4)),
            dma((4, 4)), dma((4, 4)), dma((2,)), dma((3, 2)), dma((4,)), dma((4, 4)),
            dma((3, 4)), dma, dma((2, 16)), dma((2, 16)), dma((8,)), dma((8,)), dma,
            dma((16,)), dma((16,)), dma((32,)), dma((8,)), dma((16,)), dma((16,)),
        ],
        compiler_params=pltpu.CompilerParams(
            collective_id=0, has_side_effects=True, vmem_limit_bytes=56 << 20
        ),
        name="cka",
    )(probe_states, norm_gain[None, :], gate_weight, up_weight, down_weight, route_weight)


def solution(mesh):
    return jax.shard_map(
        shards,
        mesh=mesh,
        in_specs=(
            P("tok", None),
            P(),
            P(("grp", "tok"), None),
            P(("grp", "tok"), None),
            P(("grp", "tok"), None),
            P(("grp", "tok"), None),
        ),
        out_specs=(P(("grp", "tok"), None), P()),
        check_vma=False,
    )
```

```python
import functools

import jax
import jax.numpy as jnp
from jax import lax
from jax.experimental import pallas as pl
from jax.experimental.pallas import tpu as pltpu
from jax.sharding import PartitionSpec as P

CUTS = (0, 256, 640, 1024, 2048)
F32 = jnp.float32
BF16 = jnp.bfloat16
NT = (((1,), (1,)), ((), ()))
MESH = pl.DeviceIdType.MESH
FAR_FIRST = sorted(range(1, 16), key=lambda s: -min(s, 16 - s))
TOK_FAR_FIRST = sorted(range(1, 32), key=lambda s: -min(s % 16, 16 - s % 16))
VM = pl.BlockSpec(memory_space=pltpu.VMEM)


class Place:
    def __init__(self):
        self.g = lax.axis_index("grp")
        self.t = lax.axis_index("tok")
        self.xl = self.g // 8
        self.y = (self.g // 2) % 4
        self.c = self.g % 2
        self.xh = self.t // 16
        self.z = self.t % 16
        self.q = self.t % 4
        self.h = self.t // 4
        self.base = self.h * 4
        self.owner_q = 1 + self.c
        self.owner = self.base + self.owner_q
        self.rank = (self.q + 4 - self.owner_q) % 4

    def at_y(self, step):
        return (self.xl * 8 + ((self.y + step) % 4) * 2 + self.c, self.t)

    def at_x(self, step):
        x = (self.xh * 2 + self.xl + step) % 4
        return ((x % 2) * 8 + self.y * 2 + self.c, (x // 2) * 16 + self.z)

    def at_z(self, step):
        return (self.g, self.xh * 16 + (self.z + step) % 16)

    def at_core(self):
        return (self.xl * 8 + self.y * 2 + 1 - self.c, self.t)


def push(src, dst, send, recv, device):
    return pltpu.make_async_remote_copy(
        src_ref=src, dst_ref=dst, send_sem=send, recv_sem=recv, device_id=device, device_id_type=MESH
    )


def greet(devices):
    barrier = pltpu.get_barrier_semaphore()
    for device in devices:
        pl.semaphore_signal(barrier, inc=1, device_id=device, device_id_type=MESH)
    return barrier


def cka_kernel(
    x_hbm, gain_hbm, gate_hbm, up_hbm, down_hbm, route_hbm,
    out_ref, cka_ref,
    x_ref, gain_ref, route_ref, gate_ref, up_ref, down_ref, wide_route, nrm, tok, hid, downs, routes,
    feats, column_sum, proj_column, proj_row, cen, mid, arr, folded, part, first, mine, second, rows_sum, total_ref,
    l_sem, z_send, z_recv, h_send, h_recv, y_send, y_recv, x_send, x_recv, c_send, c_recv, w_send, w_recv, d_send, d_recv,
    f_send, f_recv, a_send, a_recv, b_send, b_recv, k_sem, p_send, p_recv, s_send, s_recv, t_send, t_recv,
):
    me = Place()
    is_owner = me.rank == 0
    not_owner = jnp.logical_not(is_owner)

    loads = [
        pltpu.make_async_copy(src, dst, l_sem.at[i])
        for i, (src, dst) in enumerate(
            (
                (x_hbm, x_ref), (gain_hbm, gain_ref), (route_hbm, route_ref),
                (down_hbm, down_ref), (gate_hbm, gate_ref), (up_hbm, up_ref),
            )
        )
    ]
    for load in loads:
        load.start()

    def over_tok(step):
        return (me.g, (me.t + step) % 32)

    def over_grp(step):
        return ((me.g + step) % 16, me.t)

    def owner_in_grp(step):
        g = (me.g + step) % 16
        return g, (g, me.base + 1 + g % 2)

    def owner_in_tok(step):
        h = (me.h + step) % 8
        return h, (me.g, h * 4 + me.owner_q)

    partners = [over_tok(s) for s in range(1, 32)] + [over_grp(s) for s in range(1, 16)]
    partners += [me.at_x(3 - 2 * me.xl)]
    barrier = greet(partners)

    @pl.when(is_owner)
    def _():
        for s in range(1, 16, 2):
            pl.semaphore_signal(barrier, inc=1, device_id=owner_in_grp(s)[1], device_id_type=MESH)

    for load in loads[:3]:
        load.wait()
    states = x_ref[...].astype(F32)
    scale = lax.rsqrt(jnp.mean(states * states, axis=1, keepdims=True) + 1e-06)
    nrm[...] = (states * scale * gain_ref[...]).astype(BF16)
    wide_route[...] = jnp.broadcast_to(route_ref[...], (8, 256))
    group = me.c * 8 + me.xl * 4 + me.y
    rows = pl.ds(pl.multiple_of(me.t * 32, 32), 32)
    columns = pl.ds(pl.multiple_of(group * 128, 128), 128)
    tok[rows, columns] = nrm[:, columns]
    loads[3].wait()

    @pl.when(is_owner)
    def _():
        pl.semaphore_wait(barrier, len(partners) + 8)

    @pl.when(not_owner)
    def _():
        pl.semaphore_wait(barrier, len(partners))

    sends = []

    def start(copy):
        copy.start()
        sends.append(copy)

    for s in FAR_FIRST:
        start(push(nrm.at[:, columns], tok.at[rows, columns], z_send.at[s], z_recv.at[s], me.at_z(s)))
    for s in range(1, 16):
        source = pl.ds(pl.multiple_of((me.xh * 16 + (me.z + 16 - s) % 16) * 32, 32), 32)
        push(nrm.at[:, columns], tok.at[source, columns], z_send.at[s], z_recv.at[s], me.at_z(s)).wait_recv()

    def spot(step_x, y):
        x = (me.xh * 2 + me.xl + step_x) % 4
        row = pl.multiple_of((x // 2) * 512, 512)
        return row, pl.multiple_of((me.c * 8 + (x % 2) * 4 + y) * 128, 128)

    def y_copy(half, part, direction, source_step, slot):
        row, col = spot(2 * half, (me.y + source_step) % 4)
        start_row, count = ((0, 512), (0, 256), (256, 256))[part]
        block = tok.at[pl.ds(row + start_row, count), pl.ds(col, 128)]
        return push(block, block, y_send.at[half, slot], y_recv.at[half, slot], me.at_y(direction))

    def x_copy(slot, direction, source_step, y):
        row, col = spot(source_step, y)
        block = tok.at[pl.ds(row, 512), pl.ds(col, 128)]
        return push(block, block, x_send.at[slot, y], x_recv.at[slot, y], me.at_x(direction))

    def both_x(step_y):
        y = (me.y + step_y) % 4
        start(x_copy(0, 1, 0, y))
        start(x_copy(1, 3, 0, y))

    def core_block(step_x, core):
        x = (me.xh * 2 + me.xl + step_x) % 4
        row = pl.multiple_of((x // 2) * 512, 512)
        col = pl.multiple_of((core * 8 + (x % 2) * 4) * 128, 128)
        block = tok.at[pl.ds(row, 512), pl.ds(col, 512)]
        return push(block, block, c_send.at[step_x, 0], c_recv.at[step_x, 0], me.at_core())

    def core_piece(step_x, y, core):
        x = (me.xh * 2 + me.xl + step_x) % 4
        row = pl.multiple_of((x // 2) * 512, 512)
        col = pl.multiple_of((core * 8 + (x % 2) * 4 + y) * 128, 128)
        block = tok.at[pl.ds(row, 512), pl.ds(col, 128)]
        return push(block, block, c_send.at[step_x, y], c_recv.at[step_x, y], me.at_core())

    row, col = spot(0, me.y)
    own = tok.at[pl.ds(row, 512), pl.ds(col, 128)]
    start(push(own, own, h_send, h_recv, me.at_x(2)))
    start(y_copy(0, 0, 1, 0, 0))
    start(y_copy(0, 0, 3, 0, 1))
    both_x(0)

    owner = (me.g, me.owner)
    slot = (me.rank + 3) % 4
    down_copy = push(down_ref, downs.at[slot], w_send.at[0], w_recv.at[slot, 0], owner)
    route_copy = push(wide_route, routes.at[me.q], w_send.at[1], w_recv.at[slot, 1], owner)

    @pl.when(not_owner)
    def _():
        down_copy.start()
        route_copy.start()

    y_copy(0, 0, 1, 3, 0).wait_recv()
    start(y_copy(0, 1, 1, 3, 2))
    both_x(3)
    y_copy(0, 0, 3, 1, 1).wait_recv()
    start(y_copy(0, 2, 3, 1, 3))
    both_x(1)
    row, col = spot(2, me.y)
    other = tok.at[pl.ds(row, 512), pl.ds(col, 128)]
    push(other, other, h_send, h_recv, me.at_x(2)).wait_recv()
    start(y_copy(1, 0, 1, 0, 0))
    start(y_copy(1, 0, 3, 0, 1))
    y_copy(0, 1, 1, 2, 2).wait_recv()
    y_copy(0, 2, 3, 2, 3).wait_recv()
    both_x(2)
    start(core_block(0, me.c))
    y_copy(1, 0, 1, 3, 0).wait_recv()
    start(y_copy(1, 1, 1, 3, 2))
    y_copy(1, 0, 3, 1, 1).wait_recv()
    start(y_copy(1, 2, 3, 1, 3))
    y_copy(1, 1, 1, 2, 2).wait_recv()
    y_copy(1, 2, 3, 2, 3).wait_recv()
    start(core_block(2, me.c))

    def chunk_rows(k):
        block = (me.xh * 2 + k) % 4
        return block, pl.ds(pl.multiple_of(block * 256, 256), 256)

    def hidden_copy(k, source_slot):
        _, rows_k = chunk_rows(k)
        return push(
            hid.at[0, rows_k], hid.at[source_slot, rows_k], d_send.at[k], d_recv.at[source_slot, k], owner
        )

    def make_hidden(half):
        half_rows = pl.ds(pl.multiple_of(((me.xh + half) % 2) * 512, 512), 512)
        block = tok[half_rows, :]
        gate = lax.dot_general(block, gate_ref[...], NT, preferred_element_type=F32)
        upward = lax.dot_general(block, up_ref[...], NT, preferred_element_type=F32)
        hid[0, half_rows, :] = (gate / (1.0 + jnp.exp(-gate)) * upward).astype(BF16)

        @pl.when(not_owner)
        def _():
            for k in (2 * half, 2 * half + 1):
                hidden_copy(k, me.rank).start()

    def along_x(d):
        y = (me.y + d) % 4
        x_copy(0, 1, 3, y).wait_recv()
        start(core_piece(3, y, me.c))
        x_copy(1, 3, 1, y).wait_recv()
        start(core_piece(1, y, me.c))

    for d in (0, 3, 1, 2):
        along_x(d)
    loads[4].wait()
    loads[5].wait()
    for half, twin in ((0, 1 + 2 * me.xl), (1, 3 - 2 * me.xl)):
        core_block(2 * half, 1 - me.c).wait_recv()
        for d in (0, 3, 1, 2):
            core_piece(twin, (me.y + d) % 4, 1 - me.c).wait_recv()
        make_hidden(half)

    def feature_copy(k, part):
        block, rows_k = chunk_rows(k)
        cols = slice(CUTS[part], CUTS[part + 1])
        device = (me.g, me.base + block)
        return block, push(feats.at[rows_k, cols], out_ref.at[:, cols], f_send.at[part, k], f_recv, device)

    def ship(k, part):
        block, copy = feature_copy(k, part)

        @pl.when(block != me.q)
        def _():
            copy.start()

    def first_copy(batch, g_to, g_from, step, device):
        cols = slice(1280 * batch, 1280 * batch + 1280)
        src = cen.at[pl.ds(pl.multiple_of(g_to * 16, 16), 16), cols]
        return push(src, mid.at[g_from, :, cols], a_send.at[batch, step], a_recv.at[batch, step], device)

    def first_step(batch):
        cols = slice(1280 * batch, 1280 * batch + 1280)
        mid[me.g, :, cols] = cen[pl.ds(pl.multiple_of(me.g * 16, 16), 16), cols]
        for s in range(1, 16):
            g, device = owner_in_grp(s)
            first_copy(batch, g, me.g, s, device).start()

    def slot_of(h):
        return (
            pl.ds(pl.multiple_of((h // 4) * 8, 8), 8),
            pl.ds(pl.multiple_of((h % 4) * 640, 128), 640),
        )

    def landing(g, h):
        return arr.at[pl.ds(pl.multiple_of((g * 8 + h) * 8, 8), 8), :]

    def many(step, device):
        block = arr.at[pl.ds(0, 128), :]
        return push(block, block, b_send.at[step], b_recv.at[step], device)

    def send_on(batch, g):
        for s in (2, 6, 1, 3, 5, 7, 4):
            h, device = owner_in_tok(s)
            r, k = slot_of(h)

            @pl.when((h % 4) // 2 == batch)
            def _():
                push(mid.at[g, r, k], landing(g, me.h), b_send.at[s], b_recv.at[s], device).start()

        r, k = slot_of(me.h)

        @pl.when((me.h % 4) // 2 == batch)
        def _():
            pltpu.make_async_copy(mid.at[g, r, k], landing(g, me.h), k_sem).start()

    def part_copy(step):
        g, device = owner_in_grp(step)
        src = part.at[pl.ds(pl.multiple_of(g * 8, 8), 8), :]
        return push(src, first.at[step], p_send.at[step], p_recv.at[step], device)

    def row_copy(step):
        return push(mine, second.at[me.h], s_send.at[step], s_recv.at[me.h], over_tok(step))

    @pl.when(is_owner)
    def _():
        for j in range(1, 4):
            device = (me.g, me.base + (me.owner_q + j) % 4)
            push(down_ref, downs.at[j - 1], w_send.at[0], w_recv.at[j - 1, 0], device).wait_recv()
            push(
                wide_route, routes.at[(me.owner_q + j) % 4], w_send.at[1], w_recv.at[j - 1, 1], device
            ).wait_recv()
        routes[me.q] = wide_route[...]
        column_sum[...] = jnp.zeros_like(column_sum)

        @pl.loop(0, 4)
        def _(k):
            block, rows_k = chunk_rows(k)
            for j in range(1, 4):
                hidden_copy(k, j).wait_recv()

            route = routes[block]
            route_column = jnp.transpose(jnp.concatenate([route] * 16, axis=0))

            @pl.loop(0, 4)
            def _(n):
                cols = pl.ds(pl.multiple_of(n * 512, 512), 512)
                out = jnp.dot(hid[0, rows_k, :], down_ref[:, cols], preferred_element_type=F32)
                for j in range(1, 4):
                    out += jnp.dot(hid[j, rows_k, :], downs[j - 1, :, cols], preferred_element_type=F32)
                wide = jnp.concatenate([route_column] * 4, axis=1)
                rounded = (out * wide).astype(BF16)
                feats[rows_k, cols] = rounded
                column_sum[:, cols] += jnp.sum(rounded.astype(F32).reshape(32, 8, 512), axis=0)

        for k in range(3):
            ship(k, 0)
        mean = jnp.sum(column_sum[...], axis=0, keepdims=True) / 1024
        mean_square = jnp.sum(mean * mean, axis=1, keepdims=True)
        column_sum[...] = jnp.broadcast_to(mean, (8, 2048))

        @pl.loop(0, 4)
        def _(i):
            rows_i = pl.ds(pl.multiple_of(i * 256, 256), 256)
            total = jnp.zeros((256, 128), F32)
            for n in range(16):
                lanes = slice(n * 128, n * 128 + 128)
                total += feats[rows_i, lanes].astype(F32) * column_sum[0:1, lanes]
            projection = jnp.broadcast_to(jnp.sum(total, axis=1, keepdims=True), (256, 128))
            proj_column[rows_i, :] = projection
            proj_row[:, rows_i] = jnp.transpose(projection)[0:8, :]

        ship(3, 0)

        def gram_block(p):
            i = p % 4
            j = (i + p // 4) % 4
            rows_i = pl.ds(pl.multiple_of(i * 256, 256), 256)
            rows_j = pl.ds(pl.multiple_of(j * 256, 256), 256)
            gram = lax.dot_general(feats[rows_i, :], feats[rows_j, :], NT, preferred_element_type=F32)
            column = proj_column[rows_i, :]
            block = gram - jnp.concatenate([column, column], axis=1) - proj_row[0:1, rows_j] + mean_square
            cen[:, pl.ds(pl.multiple_of(p * 256, 256), 256)] = block.astype(BF16)

        for batch in (0, 1):
            pl.loop(5 * batch, 5 * batch + 5)(gram_block)
            first_step(batch)

        for batch in (0, 1):
            send_on(batch, me.g)

            @pl.loop(1, 16)
            def _(s):
                g, device = owner_in_grp(16 - s)
                first_copy(batch, me.g, g, s, device).wait_recv()
                send_on(batch, g)

        out_ref[...] = feats[pl.ds(pl.multiple_of(me.q * 256, 256), 256), :]
        whole = arr.at[pl.ds(0, 128), :]
        pltpu.make_async_copy(whole, whole, k_sem).wait()
        for s in range(1, 8):
            many(s, owner_in_tok(s)[1]).wait_recv()

        position = (me.h % 4) * 640 + lax.broadcasted_iota(jnp.int32, (1, 640), 1)
        weight = jnp.where(position < 1024, 1.0, 2.0)
        lane = lax.broadcasted_iota(jnp.int32, (256, 256), 1) % 8
        sublane = lax.broadcasted_iota(jnp.int32, (256, 256), 0) % 8

        pick = lax.broadcasted_iota(jnp.int32, (1024, 128), 0) // 8
        pick = (pick == lax.broadcasted_iota(jnp.int32, (1024, 128), 1)).astype(F32).astype(BF16)
        folded[...] = jnp.zeros_like(folded)
        for k in range(4):
            ship(k, 1)
        for i in range(4):
            left = (arr[256 * i : 256 * i + 256, :].astype(F32) * weight).astype(BF16)

            @pl.loop(i, 4)
            def _(j):
                rows_j = pl.ds(pl.multiple_of(j * 256, 256), 256)
                block = lax.dot_general(left, arr[rows_j, :], NT, preferred_element_type=F32)
                block = jnp.where(lane == sublane, block, 0.0)
                folded[32 * i : 32 * i + 32, rows_j] = jnp.sum(block.reshape(32, 8, 256), axis=1)

            rest = folded[32 * i : 32 * i + 32, :]
            result = jnp.zeros((32, 128), F32)
            for _ in range(3):
                top = rest.astype(BF16)
                rest = rest - top.astype(F32)
                result += jnp.dot(top, pick, preferred_element_type=F32)
            part[32 * i : 32 * i + 32, :] = result
            for g in range(4 * i, 4 * i + 4):

                @pl.when(me.g != g)
                def _():
                    part_copy((g + 16 - me.g) % 16).start()

        for k in range(4):
            ship(k, 2)
        own = part[pl.ds(pl.multiple_of(me.g * 8, 8), 8), :]
        for s in range(1, 16):
            part_copy(s).wait_recv()
            own += first[s]
        mine[...] = own
        second[me.h] = own

        for s in TOK_FAR_FIRST:
            row_copy(s).start()
        for k in range(4):
            ship(k, 3)

    for h in range(8):
        source = (me.g, h * 4 + me.owner_q)

        @pl.when(source[1] != me.t)
        def _():
            push(mine, second.at[h], s_send.at[0], s_recv.at[h], source).wait_recv()

    total = second[0]
    for h in range(1, 8):
        total += second[h]
    rows_sum[...] = total

    def total_copy(step, source):
        there = pl.ds(pl.multiple_of(source * 8, 8), 8)
        return push(rows_sum, total_ref.at[there], t_send.at[step], t_recv.at[step], over_grp(step))

    total_ref[pl.ds(pl.multiple_of(me.g * 8, 8), 8), :] = total
    for s in range(1, 16):
        total_copy(s, me.g).start()
    for s in range(1, 16):
        total_copy(s, (me.g + 16 - s) % 16).wait_recv()

    pairs = total_ref[...]
    row = lax.broadcasted_iota(jnp.int32, (128, 128), 0)
    col = lax.broadcasted_iota(jnp.int32, (128, 128), 1)
    pairs = jnp.where(row // 32 <= col // 32, pairs, jnp.transpose(pairs))
    eye = row == col
    only = jnp.where(eye, pairs, 0.0)
    down = jnp.sum(only, axis=1, keepdims=True)
    across = jnp.sum(only, axis=0, keepdims=True)
    cka_ref[...] = pairs / jnp.sqrt(down * across)

    for s in range(1, 16):
        total_copy(s, me.g).wait_send()

    @pl.when(is_owner)
    def _():
        for s in range(1, 16):
            g, device = owner_in_grp(s)
            for batch in (0, 1):
                first_copy(batch, g, me.g, s, device).wait_send()
            part_copy(s).wait_send()
        for s in range(1, 8):
            many(s, owner_in_tok(s)[1]).wait_send()

        @pl.loop(1, 32)
        def _(s):
            row_copy(s).wait_send()

        for k in range(4):
            for part in range(4):
                block, copy = feature_copy(k, part)

                @pl.when(block != me.q)
                def _():
                    copy.wait_send()

    @pl.when(not_owner)
    def _():
        down_copy.wait_send()
        route_copy.wait_send()

        @pl.loop(0, 4)
        def _(k):
            hidden_copy(k, me.rank).wait_send()

        push(feats.at[pl.ds(0, 256), :], out_ref, f_send.at[0, 0], f_recv, owner).wait_recv()

    for copy in sends:
        copy.wait_send()


def shards(probe_states, norm_gain, gate_weight, up_weight, down_weight, route_weight):
    dma = pltpu.SemaphoreType.DMA
    hbm = pl.BlockSpec(memory_space=pltpu.HBM)
    return pl.pallas_call(
        cka_kernel,
        out_shape=(
            jax.ShapeDtypeStruct((256, 2048), BF16),
            jax.ShapeDtypeStruct((128, 128), F32),
        ),
        in_specs=[hbm] * 6,
        out_specs=(VM, VM),
        scratch_shapes=[
            pltpu.VMEM((32, 2048), BF16),
            pltpu.VMEM((1, 2048), F32),
            pltpu.VMEM((1, 256), F32),
            pltpu.VMEM((192, 2048), BF16),
            pltpu.VMEM((192, 2048), BF16),
            pltpu.VMEM((192, 2048), BF16),
            pltpu.VMEM((8, 256), F32),
            pltpu.VMEM((32, 2048), BF16),
            pltpu.VMEM((1024, 2048), BF16),
            pltpu.VMEM((4, 1024, 192), BF16),
            pltpu.VMEM((3, 192, 2048), BF16),
            pltpu.VMEM((4, 8, 256), F32),
            pltpu.VMEM((1024, 2048), BF16),
            pltpu.VMEM((8, 2048), F32),
            pltpu.VMEM((1024, 128), F32),
            pltpu.VMEM((8, 1024), F32),
            pltpu.VMEM((256, 2560), BF16),
            pltpu.VMEM((16, 16, 2560), BF16),
            pltpu.VMEM((1024, 640), BF16),
            pltpu.VMEM((128, 1024), F32),
            pltpu.VMEM((128, 128), F32),
            pltpu.VMEM((16, 8, 128), F32),
            pltpu.VMEM((8, 128), F32),
            pltpu.VMEM((8, 8, 128), F32),
            pltpu.VMEM((8, 128), F32),
            pltpu.VMEM((128, 128), F32),
            dma((6,)), dma((16,)), dma((16,)), dma, dma, dma((2, 4)), dma((2, 4)), dma((2, 4)), dma((2, 4)),
            dma((4, 4)), dma((4, 4)), dma((2,)), dma((3, 2)), dma((4,)), dma((4, 4)),
            dma((4, 4)), dma, dma((2, 16)), dma((2, 16)), dma((8,)), dma((8,)), dma,
            dma((16,)), dma((16,)), dma((32,)), dma((8,)), dma((16,)), dma((16,)),
        ],
        compiler_params=pltpu.CompilerParams(
            collective_id=0, has_side_effects=True, vmem_limit_bytes=56 << 20
        ),
        name="cka",
    )(probe_states, norm_gain[None, :], gate_weight, up_weight, down_weight, route_weight)


def solution(mesh):
    return jax.shard_map(
        shards,
        mesh=mesh,
        in_specs=(
            P("tok", None),
            P(),
            P(("grp", "tok"), None),
            P(("grp", "tok"), None),
            P(("grp", "tok"), None),
            P(("grp", "tok"), None),
        ),
        out_specs=(P(("grp", "tok"), None), P()),
        check_vma=False,
    )
```

```python
import functools

import jax
import jax.numpy as jnp
from jax import lax
from jax.experimental import pallas as pl
from jax.experimental.pallas import tpu as pltpu
from jax.sharding import PartitionSpec as P

CUTS = (0, 256, 640, 1024, 2048)
F32 = jnp.float32
BF16 = jnp.bfloat16
NT = (((1,), (1,)), ((), ()))
MESH = pl.DeviceIdType.MESH
FAR_FIRST = sorted(range(1, 16), key=lambda s: -min(s, 16 - s))
TOK_FAR_FIRST = sorted(range(1, 32), key=lambda s: -min(s % 16, 16 - s % 16))
VM = pl.BlockSpec(memory_space=pltpu.VMEM)


class Place:
    def __init__(self):
        self.g = lax.axis_index("grp")
        self.t = lax.axis_index("tok")
        self.xl = self.g // 8
        self.y = (self.g // 2) % 4
        self.c = self.g % 2
        self.xh = self.t // 16
        self.z = self.t % 16
        self.q = self.t % 4
        self.h = self.t // 4
        self.base = self.h * 4
        self.owner_q = 1 + self.c
        self.owner = self.base + self.owner_q
        self.rank = (self.q + 4 - self.owner_q) % 4

    def at_y(self, step):
        return (self.xl * 8 + ((self.y + step) % 4) * 2 + self.c, self.t)

    def at_x(self, step):
        x = (self.xh * 2 + self.xl + step) % 4
        return ((x % 2) * 8 + self.y * 2 + self.c, (x // 2) * 16 + self.z)

    def at_z(self, step):
        return (self.g, self.xh * 16 + (self.z + step) % 16)

    def at_core(self):
        return (self.xl * 8 + self.y * 2 + 1 - self.c, self.t)


def push(src, dst, send, recv, device):
    return pltpu.make_async_remote_copy(
        src_ref=src, dst_ref=dst, send_sem=send, recv_sem=recv, device_id=device, device_id_type=MESH
    )


def greet(devices):
    barrier = pltpu.get_barrier_semaphore()
    for device in devices:
        pl.semaphore_signal(barrier, inc=1, device_id=device, device_id_type=MESH)
    return barrier


def cka_kernel(
    x_hbm, gain_hbm, gate_hbm, up_hbm, down_hbm, route_hbm,
    out_ref, cka_ref,
    x_ref, gain_ref, route_ref, gate_ref, up_ref, down_ref, wide_route, nrm, tok, hid, downs, routes,
    feats, column_sum, proj_column, proj_row, cen, mid, arr, folded, part, first, mine, second, rows_sum, total_ref,
    l_sem, z_send, z_recv, h_send, h_recv, y_send, y_recv, x_send, x_recv, c_send, c_recv, w_send, w_recv, d_send, d_recv,
    f_send, f_recv, a_send, a_recv, b_send, b_recv, k_sem, p_send, p_recv, s_send, s_recv, t_send, t_recv,
):
    me = Place()
    is_owner = me.rank == 0
    not_owner = jnp.logical_not(is_owner)

    loads = [
        pltpu.make_async_copy(src, dst, l_sem.at[i])
        for i, (src, dst) in enumerate(
            (
                (x_hbm, x_ref), (gain_hbm, gain_ref), (route_hbm, route_ref),
                (down_hbm, down_ref), (gate_hbm, gate_ref), (up_hbm, up_ref),
            )
        )
    ]
    for load in loads:
        load.start()

    def over_tok(step):
        return (me.g, (me.t + step) % 32)

    def over_grp(step):
        return ((me.g + step) % 16, me.t)

    def owner_in_grp(step):
        g = (me.g + step) % 16
        return g, (g, me.base + 1 + g % 2)

    def owner_in_tok(step):
        h = (me.h + step) % 8
        return h, (me.g, h * 4 + me.owner_q)

    partners = [over_tok(s) for s in range(1, 32)] + [over_grp(s) for s in range(1, 16)]
    partners += [me.at_x(3 - 2 * me.xl)]
    barrier = greet(partners)

    @pl.when(is_owner)
    def _():
        for s in range(1, 16, 2):
            pl.semaphore_signal(barrier, inc=1, device_id=owner_in_grp(s)[1], device_id_type=MESH)

    for load in loads[:3]:
        load.wait()
    states = x_ref[...].astype(F32)
    scale = lax.rsqrt(jnp.mean(states * states, axis=1, keepdims=True) + 1e-06)
    nrm[...] = (states * scale * gain_ref[...]).astype(BF16)
    wide_route[...] = jnp.broadcast_to(route_ref[...], (8, 256))
    group = me.c * 8 + me.xl * 4 + me.y
    rows = pl.ds(pl.multiple_of(me.t * 32, 32), 32)
    columns = pl.ds(pl.multiple_of(group * 128, 128), 128)
    tok[rows, columns] = nrm[:, columns]
    loads[3].wait()

    @pl.when(is_owner)
    def _():
        pl.semaphore_wait(barrier, len(partners) + 8)

    @pl.when(not_owner)
    def _():
        pl.semaphore_wait(barrier, len(partners))

    sends = []

    def start(copy):
        copy.start()
        sends.append(copy)

    for s in FAR_FIRST:
        start(push(nrm.at[:, columns], tok.at[rows, columns], z_send.at[s], z_recv.at[s], me.at_z(s)))
    for s in range(1, 16):
        source = pl.ds(pl.multiple_of((me.xh * 16 + (me.z + 16 - s) % 16) * 32, 32), 32)
        push(nrm.at[:, columns], tok.at[source, columns], z_send.at[s], z_recv.at[s], me.at_z(s)).wait_recv()

    def spot(step_x, y):
        x = (me.xh * 2 + me.xl + step_x) % 4
        row = pl.multiple_of((x // 2) * 512, 512)
        return row, pl.multiple_of((me.c * 8 + (x % 2) * 4 + y) * 128, 128)

    def y_copy(half, part, direction, source_step, slot):
        row, col = spot(2 * half, (me.y + source_step) % 4)
        start_row, count = ((0, 512), (0, 256), (256, 256))[part]
        block = tok.at[pl.ds(row + start_row, count), pl.ds(col, 128)]
        return push(block, block, y_send.at[half, slot], y_recv.at[half, slot], me.at_y(direction))

    def x_copy(slot, direction, source_step, y):
        row, col = spot(source_step, y)
        block = tok.at[pl.ds(row, 512), pl.ds(col, 128)]
        return push(block, block, x_send.at[slot, y], x_recv.at[slot, y], me.at_x(direction))

    def both_x(step_y):
        y = (me.y + step_y) % 4
        start(x_copy(0, 1, 0, y))
        start(x_copy(1, 3, 0, y))

    def core_block(step_x, core):
        x = (me.xh * 2 + me.xl + step_x) % 4
        row = pl.multiple_of((x // 2) * 512, 512)
        col = pl.multiple_of((core * 8 + (x % 2) * 4) * 128, 128)
        block = tok.at[pl.ds(row, 512), pl.ds(col, 512)]
        return push(block, block, c_send.at[step_x, 0], c_recv.at[step_x, 0], me.at_core())

    def core_piece(step_x, y, core):
        x = (me.xh * 2 + me.xl + step_x) % 4
        row = pl.multiple_of((x // 2) * 512, 512)
        col = pl.multiple_of((core * 8 + (x % 2) * 4 + y) * 128, 128)
        block = tok.at[pl.ds(row, 512), pl.ds(col, 128)]
        return push(block, block, c_send.at[step_x, y], c_recv.at[step_x, y], me.at_core())

    row, col = spot(0, me.y)
    own = tok.at[pl.ds(row, 512), pl.ds(col, 128)]
    start(push(own, own, h_send, h_recv, me.at_x(2)))
    start(y_copy(0, 0, 1, 0, 0))
    start(y_copy(0, 0, 3, 0, 1))
    both_x(0)

    owner = (me.g, me.owner)
    slot = (me.rank + 3) % 4
    down_copy = push(down_ref, downs.at[slot], w_send.at[0], w_recv.at[slot, 0], owner)
    route_copy = push(wide_route, routes.at[me.q], w_send.at[1], w_recv.at[slot, 1], owner)

    @pl.when(not_owner)
    def _():
        down_copy.start()
        route_copy.start()

    y_copy(0, 0, 1, 3, 0).wait_recv()
    start(y_copy(0, 1, 1, 3, 2))
    both_x(3)
    y_copy(0, 0, 3, 1, 1).wait_recv()
    start(y_copy(0, 2, 3, 1, 3))
    both_x(1)
    row, col = spot(2, me.y)
    other = tok.at[pl.ds(row, 512), pl.ds(col, 128)]
    push(other, other, h_send, h_recv, me.at_x(2)).wait_recv()
    start(y_copy(1, 0, 1, 0, 0))
    start(y_copy(1, 0, 3, 0, 1))
    y_copy(0, 1, 1, 2, 2).wait_recv()
    y_copy(0, 2, 3, 2, 3).wait_recv()
    both_x(2)
    start(core_block(0, me.c))
    y_copy(1, 0, 1, 3, 0).wait_recv()
    start(y_copy(1, 1, 1, 3, 2))
    y_copy(1, 0, 3, 1, 1).wait_recv()
    start(y_copy(1, 2, 3, 1, 3))
    y_copy(1, 1, 1, 2, 2).wait_recv()
    y_copy(1, 2, 3, 2, 3).wait_recv()
    start(core_block(2, me.c))

    def chunk_rows(k):
        block = (me.xh * 2 + k) % 4
        return block, pl.ds(pl.multiple_of(block * 256, 256), 256)

    def hidden_copy(k, source_slot):
        _, rows_k = chunk_rows(k)
        return push(
            hid.at[0, rows_k], hid.at[source_slot, rows_k], d_send.at[k], d_recv.at[source_slot, k], owner
        )

    def make_hidden(half):
        for k in (2 * half, 2 * half + 1):
            _, rows_k = chunk_rows(k)
            block = tok[rows_k, :]
            gate = lax.dot_general(block, gate_ref[...], NT, preferred_element_type=F32)
            upward = lax.dot_general(block, up_ref[...], NT, preferred_element_type=F32)
            hid[0, rows_k, :] = (gate / (1.0 + jnp.exp(-gate)) * upward).astype(BF16)

            @pl.when(not_owner)
            def _():
                hidden_copy(k, me.rank).start()

    def along_x(d):
        y = (me.y + d) % 4
        x_copy(0, 1, 3, y).wait_recv()
        start(core_piece(3, y, me.c))
        x_copy(1, 3, 1, y).wait_recv()
        start(core_piece(1, y, me.c))

    for d in (0, 3, 1, 2):
        along_x(d)
    loads[4].wait()
    loads[5].wait()
    for half, twin in ((0, 1 + 2 * me.xl), (1, 3 - 2 * me.xl)):
        core_block(2 * half, 1 - me.c).wait_recv()
        for d in (0, 3, 1, 2):
            core_piece(twin, (me.y + d) % 4, 1 - me.c).wait_recv()
        make_hidden(half)

    def feature_copy(k, part):
        block, rows_k = chunk_rows(k)
        cols = slice(CUTS[part], CUTS[part + 1])
        device = (me.g, me.base + block)
        return block, push(feats.at[rows_k, cols], out_ref.at[:, cols], f_send.at[part, k], f_recv, device)

    def ship(k, part):
        block, copy = feature_copy(k, part)

        @pl.when(block != me.q)
        def _():
            copy.start()

    def first_copy(batch, g_to, g_from, step, device):
        cols = slice(1280 * batch, 1280 * batch + 1280)
        src = cen.at[pl.ds(pl.multiple_of(g_to * 16, 16), 16), cols]
        return push(src, mid.at[g_from, :, cols], a_send.at[batch, step], a_recv.at[batch, step], device)

    def first_step(batch):
        cols = slice(1280 * batch, 1280 * batch + 1280)
        mid[me.g, :, cols] = cen[pl.ds(pl.multiple_of(me.g * 16, 16), 16), cols]
        for s in range(1, 16):
            g, device = owner_in_grp(s)
            first_copy(batch, g, me.g, s, device).start()

    def slot_of(h):
        return (
            pl.ds(pl.multiple_of((h // 4) * 8, 8), 8),
            pl.ds(pl.multiple_of((h % 4) * 640, 128), 640),
        )

    def landing(g, h):
        return arr.at[pl.ds(pl.multiple_of((g * 8 + h) * 8, 8), 8), :]

    def many(step, device):
        block = arr.at[pl.ds(0, 128), :]
        return push(block, block, b_send.at[step], b_recv.at[step], device)

    def send_on(batch, g):
        for s in (2, 6, 1, 3, 5, 7, 4):
            h, device = owner_in_tok(s)
            r, k = slot_of(h)

            @pl.when((h % 4) // 2 == batch)
            def _():
                push(mid.at[g, r, k], landing(g, me.h), b_send.at[s], b_recv.at[s], device).start()

        r, k = slot_of(me.h)

        @pl.when((me.h % 4) // 2 == batch)
        def _():
            pltpu.make_async_copy(mid.at[g, r, k], landing(g, me.h), k_sem).start()

    def part_copy(step):
        g, device = owner_in_grp(step)
        src = part.at[pl.ds(pl.multiple_of(g * 8, 8), 8), :]
        return push(src, first.at[step], p_send.at[step], p_recv.at[step], device)

    def row_copy(step):
        return push(mine, second.at[me.h], s_send.at[step], s_recv.at[me.h], over_tok(step))

    @pl.when(is_owner)
    def _():
        for j in range(1, 4):
            device = (me.g, me.base + (me.owner_q + j) % 4)
            push(down_ref, downs.at[j - 1], w_send.at[0], w_recv.at[j - 1, 0], device).wait_recv()
            push(
                wide_route, routes.at[(me.owner_q + j) % 4], w_send.at[1], w_recv.at[j - 1, 1], device
            ).wait_recv()
        routes[me.q] = wide_route[...]
        column_sum[...] = jnp.zeros_like(column_sum)

        @pl.loop(0, 4)
        def _(k):
            block, rows_k = chunk_rows(k)
            for j in range(1, 4):
                hidden_copy(k, j).wait_recv()

            route = routes[block]
            route_column = jnp.transpose(jnp.concatenate([route] * 16, axis=0))

            @pl.loop(0, 4)
            def _(n):
                cols = pl.ds(pl.multiple_of(n * 512, 512), 512)
                out = jnp.dot(hid[0, rows_k, :], down_ref[:, cols], preferred_element_type=F32)
                for j in range(1, 4):
                    out += jnp.dot(hid[j, rows_k, :], downs[j - 1, :, cols], preferred_element_type=F32)
                wide = jnp.concatenate([route_column] * 4, axis=1)
                rounded = (out * wide).astype(BF16)
                feats[rows_k, cols] = rounded
                column_sum[:, cols] += jnp.sum(rounded.astype(F32).reshape(32, 8, 512), axis=0)

        for k in range(3):
            ship(k, 0)
        mean = jnp.sum(column_sum[...], axis=0, keepdims=True) / 1024
        mean_square = jnp.sum(mean * mean, axis=1, keepdims=True)
        column_sum[...] = jnp.broadcast_to(mean, (8, 2048))

        @pl.loop(0, 4)
        def _(i):
            rows_i = pl.ds(pl.multiple_of(i * 256, 256), 256)
            total = jnp.zeros((256, 128), F32)
            for n in range(16):
                lanes = slice(n * 128, n * 128 + 128)
                total += feats[rows_i, lanes].astype(F32) * column_sum[0:1, lanes]
            projection = jnp.broadcast_to(jnp.sum(total, axis=1, keepdims=True), (256, 128))
            proj_column[rows_i, :] = projection
            proj_row[:, rows_i] = jnp.transpose(projection)[0:8, :]

        ship(3, 0)

        def gram_block(p):
            i = p % 4
            j = (i + p // 4) % 4
            rows_i = pl.ds(pl.multiple_of(i * 256, 256), 256)
            rows_j = pl.ds(pl.multiple_of(j * 256, 256), 256)
            gram = lax.dot_general(feats[rows_i, :], feats[rows_j, :], NT, preferred_element_type=F32)
            column = proj_column[rows_i, :]
            block = gram - jnp.concatenate([column, column], axis=1) - proj_row[0:1, rows_j] + mean_square
            cen[:, pl.ds(pl.multiple_of(p * 256, 256), 256)] = block.astype(BF16)

        for batch in (0, 1):
            pl.loop(5 * batch, 5 * batch + 5)(gram_block)
            first_step(batch)

        for batch in (0, 1):
            send_on(batch, me.g)

            @pl.loop(1, 16)
            def _(s):
                g, device = owner_in_grp(16 - s)
                first_copy(batch, me.g, g, s, device).wait_recv()
                send_on(batch, g)

        out_ref[...] = feats[pl.ds(pl.multiple_of(me.q * 256, 256), 256), :]
        whole = arr.at[pl.ds(0, 128), :]
        pltpu.make_async_copy(whole, whole, k_sem).wait()
        for s in range(1, 8):
            many(s, owner_in_tok(s)[1]).wait_recv()

        position = (me.h % 4) * 640 + lax.broadcasted_iota(jnp.int32, (1, 640), 1)
        weight = jnp.where(position < 1024, 1.0, 2.0)
        lane = lax.broadcasted_iota(jnp.int32, (256, 256), 1) % 8
        sublane = lax.broadcasted_iota(jnp.int32, (256, 256), 0) % 8

        pick = lax.broadcasted_iota(jnp.int32, (1024, 128), 0) // 8
        pick = (pick == lax.broadcasted_iota(jnp.int32, (1024, 128), 1)).astype(F32).astype(BF16)
        folded[...] = jnp.zeros_like(folded)
        for k in range(4):
            ship(k, 1)
        for i in range(4):
            left = (arr[256 * i : 256 * i + 256, :].astype(F32) * weight).astype(BF16)

            @pl.loop(i, 4)
            def _(j):
                rows_j = pl.ds(pl.multiple_of(j * 256, 256), 256)
                block = lax.dot_general(left, arr[rows_j, :], NT, preferred_element_type=F32)
                block = jnp.where(lane == sublane, block, 0.0)
                folded[32 * i : 32 * i + 32, rows_j] = jnp.sum(block.reshape(32, 8, 256), axis=1)

            rest = folded[32 * i : 32 * i + 32, :]
            result = jnp.zeros((32, 128), F32)
            for _ in range(3):
                top = rest.astype(BF16)
                rest = rest - top.astype(F32)
                result += jnp.dot(top, pick, preferred_element_type=F32)
            part[32 * i : 32 * i + 32, :] = result
            for g in range(4 * i, 4 * i + 4):

                @pl.when(me.g != g)
                def _():
                    part_copy((g + 16 - me.g) % 16).start()

        for k in range(4):
            ship(k, 2)
        own = part[pl.ds(pl.multiple_of(me.g * 8, 8), 8), :]
        for s in range(1, 16):
            part_copy(s).wait_recv()
            own += first[s]
        mine[...] = own
        second[me.h] = own

        for s in TOK_FAR_FIRST:
            row_copy(s).start()
        for k in range(4):
            ship(k, 3)

    for h in range(8):
        source = (me.g, h * 4 + me.owner_q)

        @pl.when(source[1] != me.t)
        def _():
            push(mine, second.at[h], s_send.at[0], s_recv.at[h], source).wait_recv()

    total = second[0]
    for h in range(1, 8):
        total += second[h]
    rows_sum[...] = total

    def total_copy(step, source):
        there = pl.ds(pl.multiple_of(source * 8, 8), 8)
        return push(rows_sum, total_ref.at[there], t_send.at[step], t_recv.at[step], over_grp(step))

    total_ref[pl.ds(pl.multiple_of(me.g * 8, 8), 8), :] = total
    for s in range(1, 16):
        total_copy(s, me.g).start()
    for s in range(1, 16):
        total_copy(s, (me.g + 16 - s) % 16).wait_recv()

    pairs = total_ref[...]
    row = lax.broadcasted_iota(jnp.int32, (128, 128), 0)
    col = lax.broadcasted_iota(jnp.int32, (128, 128), 1)
    pairs = jnp.where(row // 32 <= col // 32, pairs, jnp.transpose(pairs))
    eye = row == col
    only = jnp.where(eye, pairs, 0.0)
    down = jnp.sum(only, axis=1, keepdims=True)
    across = jnp.sum(only, axis=0, keepdims=True)
    cka_ref[...] = pairs / jnp.sqrt(down * across)

    for s in range(1, 16):
        total_copy(s, me.g).wait_send()

    @pl.when(is_owner)
    def _():
        for s in range(1, 16):
            g, device = owner_in_grp(s)
            for batch in (0, 1):
                first_copy(batch, g, me.g, s, device).wait_send()
            part_copy(s).wait_send()
        for s in range(1, 8):
            many(s, owner_in_tok(s)[1]).wait_send()

        @pl.loop(1, 32)
        def _(s):
            row_copy(s).wait_send()

        for k in range(4):
            for part in range(4):
                block, copy = feature_copy(k, part)

                @pl.when(block != me.q)
                def _():
                    copy.wait_send()

    @pl.when(not_owner)
    def _():
        down_copy.wait_send()
        route_copy.wait_send()

        @pl.loop(0, 4)
        def _(k):
            hidden_copy(k, me.rank).wait_send()

        push(feats.at[pl.ds(0, 256), :], out_ref, f_send.at[0, 0], f_recv, owner).wait_recv()

    for copy in sends:
        copy.wait_send()


def shards(probe_states, norm_gain, gate_weight, up_weight, down_weight, route_weight):
    dma = pltpu.SemaphoreType.DMA
    hbm = pl.BlockSpec(memory_space=pltpu.HBM)
    return pl.pallas_call(
        cka_kernel,
        out_shape=(
            jax.ShapeDtypeStruct((256, 2048), BF16),
            jax.ShapeDtypeStruct((128, 128), F32),
        ),
        in_specs=[hbm] * 6,
        out_specs=(VM, VM),
        scratch_shapes=[
            pltpu.VMEM((32, 2048), BF16),
            pltpu.VMEM((1, 2048), F32),
            pltpu.VMEM((1, 256), F32),
            pltpu.VMEM((192, 2048), BF16),
            pltpu.VMEM((192, 2048), BF16),
            pltpu.VMEM((192, 2048), BF16),
            pltpu.VMEM((8, 256), F32),
            pltpu.VMEM((32, 2048), BF16),
            pltpu.VMEM((1024, 2048), BF16),
            pltpu.VMEM((4, 1024, 192), BF16),
            pltpu.VMEM((3, 192, 2048), BF16),
            pltpu.VMEM((4, 8, 256), F32),
            pltpu.VMEM((1024, 2048), BF16),
            pltpu.VMEM((8, 2048), F32),
            pltpu.VMEM((1024, 128), F32),
            pltpu.VMEM((8, 1024), F32),
            pltpu.VMEM((256, 2560), BF16),
            pltpu.VMEM((16, 16, 2560), BF16),
            pltpu.VMEM((1024, 640), BF16),
            pltpu.VMEM((128, 1024), F32),
            pltpu.VMEM((128, 128), F32),
            pltpu.VMEM((16, 8, 128), F32),
            pltpu.VMEM((8, 128), F32),
            pltpu.VMEM((8, 8, 128), F32),
            pltpu.VMEM((8, 128), F32),
            pltpu.VMEM((128, 128), F32),
            dma((6,)), dma((16,)), dma((16,)), dma, dma, dma((2, 4)), dma((2, 4)), dma((2, 4)), dma((2, 4)),
            dma((4, 4)), dma((4, 4)), dma((2,)), dma((3, 2)), dma((4,)), dma((4, 4)),
            dma((4, 4)), dma, dma((2, 16)), dma((2, 16)), dma((8,)), dma((8,)), dma,
            dma((16,)), dma((16,)), dma((32,)), dma((8,)), dma((16,)), dma((16,)),
        ],
        compiler_params=pltpu.CompilerParams(
            collective_id=0, has_side_effects=True, vmem_limit_bytes=56 << 20
        ),
        name="cka",
    )(probe_states, norm_gain[None, :], gate_weight, up_weight, down_weight, route_weight)


def solution(mesh):
    return jax.shard_map(
        shards,
        mesh=mesh,
        in_specs=(
            P("tok", None),
            P(),
            P(("grp", "tok"), None),
            P(("grp", "tok"), None),
            P(("grp", "tok"), None),
            P(("grp", "tok"), None),
        ),
        out_specs=(P(("grp", "tok"), None), P()),
        check_vma=False,
    )
```
